768 devices in a mesh: seq: 96 (over x, z, core), head: 8 (over y).
Axes of the slice: x: 4, y: 8, z: 12, core: 2. Of those that a mesh axis runs over, the one named last changes fastest.
Arguments:
- query_rows: bfloat16 [24576, 4096], P('seq', 'head'), may hold values from -6 to 6
- key_rows: bfloat16 [24576, 4096], P('seq', 'head'), may hold values from -6 to 6
- value_rows: bfloat16 [24576, 4096], P('seq', 'head'), may hold values from -150 to 150
- log_decay: float32 [32, 24576], P('head', 'seq'), may hold values from -3 to 0
- out_grad: bfloat16 [24576, 4096], P('seq', 'head'), may hold values from -6 to 6
- norm_gain: float32 [4096], P('head'), may hold values from 0.1 to 1.9
- state_in: float32 [32, 128, 128], P('head'), may hold values from -96 to 96
- state_out_grad: float32 [32, 128, 128], P('head'), may hold values from -0.4375 to 0.4375
Outputs:
- query_grad: bfloat16 [24576, 4096], P('seq', 'head')
- key_grad: bfloat16 [24576, 4096], P('seq', 'head')
- value_grad: bfloat16 [24576, 4096], P('seq', 'head')
- state_in_grad: float32 [32, 128, 128], P('head')
The draws below stay inside these ranges and needn't reach their ends.
All inputs are finite; a program needn't handle non-finite values.
Results may differ from the reference program's by a relative error of at most 0.0059.
Values sent between devices are 32-bit elements; how exact they have to be, the bound alone decides.
A program may use at most 128 MiB of HBM per device.

```python
import jax
import jax.numpy as jnp
from jax import lax

HEAD_COUNT = 32
DH = 128
TOK_DEV = 256
SLAB_TOKENS = 24576


def draw_value_rows(key, part):
    random_keys = jax.random.split(key, 3)
    head_position = (jnp.arange(HEAD_COUNT) + jax.random.uniform(random_keys[0], (HEAD_COUNT,))) / HEAD_COUNT
    head_scale = jnp.repeat(jnp.power(10.0, head_position), DH)
    token_scale = jnp.exp(jax.random.uniform(random_keys[1], (SLAB_TOKENS, 1), minval=0.0, maxval=jnp.log(10.0)))
    base_rows = jnp.clip(jax.random.normal(random_keys[2], (SLAB_TOKENS, HEAD_COUNT * DH)), -6.0, 6.0)
    return (0.25 * base_rows * head_scale[None, :] * token_scale).astype(jnp.bfloat16)


def draw_log_decay(key, part):
    random_keys = jax.random.split(key, 7)
    slow_share = 0.5
    is_slow = jax.random.uniform(random_keys[0], (HEAD_COUNT,)) < slow_share
    slow_rate = jnp.exp(jax.random.uniform(random_keys[1], (HEAD_COUNT,), minval=jnp.log(0.05), maxval=jnp.log(0.3))) / SLAB_TOKENS
    fast_low = jnp.maximum(1.0 / 50.0, 4.0 / TOK_DEV)
    fast_high = jnp.maximum(1.0 / 30.0, 6.0 / TOK_DEV)
    fast_rate = jnp.exp(jax.random.uniform(random_keys[2], (HEAD_COUNT,), minval=jnp.log(fast_low), maxval=jnp.log(fast_high)))
    baseline_rate = jnp.where(is_slow, slow_rate, fast_rate)
    segment_count = SLAB_TOKENS // TOK_DEV
    segment_scale = jnp.exp(jax.random.uniform(random_keys[3], (HEAD_COUNT, segment_count), minval=-jnp.log(2.0), maxval=jnp.log(2.0)))
    whole_segment = jnp.repeat(segment_scale, TOK_DEV, axis=1)
    token_noise = jnp.exp(jax.random.uniform(random_keys[4], (HEAD_COUNT, SLAB_TOKENS), minval=jnp.log(0.7), maxval=jnp.log(1.4)))
    spike_positions = jax.random.randint(random_keys[5], (HEAD_COUNT, 2), 0, SLAB_TOKENS)
    spike_loss = jax.random.uniform(random_keys[6], (HEAD_COUNT, 2), minval=jnp.log(0.5), maxval=jnp.log(0.8))
    token_places = jnp.arange(SLAB_TOKENS)
    spike_events = jnp.sum(jnp.where(token_places[None, :, None] == spike_positions[:, None, :], spike_loss[:, None, :], 0.0), axis=2)
    return (-baseline_rate[:, None] * whole_segment * token_noise + spike_events).astype(jnp.float32)


def shard_levels(stream_key, shape, cuts, least, high):
    def one(position, blocks):
        steps = jax.random.uniform(jax.random.fold_in(jax.random.fold_in(stream_key, 6), position), (blocks,), jnp.float32, least / len(cuts), high / len(cuts))
        return jnp.repeat(jnp.exp(steps), shape[position] // blocks).reshape((-1,) + (1,) * (len(shape) - position - 1))

    factor_of = one(*cuts[0])
    for cut in cuts[1:]:
        factor_of = factor_of * one(*cut)
    return factor_of


def noise(rng, shape, scale, most, cuts=(), dtype=jnp.bfloat16):
    gain = shard_levels(rng, shape, cuts, -0.22, 0.18) if cuts else 1.0
    result = jax.random.normal(rng, shape, jnp.float32) * scale * gain
    return jnp.minimum(jnp.maximum(result, -most), most).astype(dtype)


def setup_inputs(seed: int = 0) -> dict:
    seeds = jax.random.split(jax.random.key(seed), 9)
    query_rows = noise(seeds[0], (SLAB_TOKENS, HEAD_COUNT * DH), 1.0, 6.0, ((0, 96), (1, 8)))
    key_rows = noise(seeds[1], (SLAB_TOKENS, HEAD_COUNT * DH), 1.0, 6.0, ((0, 96), (1, 8)))
    value_rows = draw_value_rows(jax.random.fold_in(seeds[8], 71), 0)
    log_decay = draw_log_decay(jax.random.fold_in(seeds[8], 71), 0)
    out_grad = noise(seeds[4], (SLAB_TOKENS, HEAD_COUNT * DH), 1.0, 6.0, ((0, 96), (1, 8)))
    norm_gain = jnp.clip(1.0 + 0.18 * jax.random.normal(seeds[5], (HEAD_COUNT * DH,), jnp.float32), 0.1, 1.9)
    state_in = noise(seeds[6], (HEAD_COUNT, DH, DH), 16.0, 96.0, ((0, 8),), jnp.float32)
    state_out_grad = noise(seeds[7], (HEAD_COUNT, DH, DH), 0.03, 0.4375, ((0, 8),), jnp.float32)
    return dict(query_rows=query_rows, key_rows=key_rows, value_rows=value_rows, log_decay=log_decay, out_grad=out_grad, norm_gain=norm_gain, state_in=state_in, state_out_grad=state_out_grad)


EPSILON = 1e-06

def round_bf(values):
    return lax.optimization_barrier(values.astype(jnp.bfloat16)).astype(jnp.float32)

def decay_tables(decay_rows):
    cum_log = jnp.cumsum(decay_rows, axis=1)
    block_log = cum_log[:, -1]
    length = decay_rows.shape[1]
    causal = jnp.arange(length)[:, None] >= jnp.arange(length)[None, :]
    spread = cum_log[:, :, None] - cum_log[:, None, :]
    decay_mat = jnp.where(causal[None], jnp.exp(jnp.minimum(spread, 0.0)), 0.0)
    return (cum_log, block_log, decay_mat)

def reference(query_rows, key_rows, value_rows, log_decay, out_grad, norm_gain, state_in, state_out_grad):
    block_count = SLAB_TOKENS // TOK_DEV
    feature_count = HEAD_COUNT * DH
    block_shape = (block_count, TOK_DEV, HEAD_COUNT, DH)
    query_blocks = query_rows.reshape(block_shape)
    key_blocks = key_rows.reshape(block_shape)
    value_blocks = value_rows.reshape(block_shape)
    grad_blocks = out_grad.reshape(block_count, TOK_DEV, feature_count)
    decay_blocks = log_decay.reshape(HEAD_COUNT, block_count, TOK_DEV).transpose(1, 0, 2)

    def forward_step(states_prev, inputs):
        query_heads, key_heads, value_heads, grad_rows, decay_rows = inputs
        cum_log, block_log, decay_mat = decay_tables(decay_rows)
        query_f = query_heads.astype(jnp.float32)
        key_f = key_heads.astype(jnp.float32)
        value_f = value_heads.astype(jnp.float32)
        growth = jnp.exp(cum_log).T[:, :, None]
        shrink = jnp.exp(block_log[:, None] - cum_log).T[:, :, None]
        states_bf = round_bf(states_prev)
        weights = round_bf(jnp.einsum('thd,shd->hts', query_f, key_f) * decay_mat)
        attended = jnp.einsum('hts,shd->thd', weights, value_f) + growth * jnp.einsum('thd,hde->the', query_f, states_bf)
        flat_rows = attended.reshape(TOK_DEV, feature_count)
        inv_rms = lax.rsqrt(lax.optimization_barrier(jnp.mean(flat_rows * flat_rows, axis=1)) + EPSILON)
        gained = norm_gain[None, :] * grad_rows.astype(jnp.float32)
        inner = lax.optimization_barrier(jnp.sum(gained * flat_rows, axis=1))
        attn_grad = round_bf(gained * inv_rms[:, None] - flat_rows * (inner * inv_rms ** 3 / feature_count)[:, None])
        grad_heads = attn_grad.reshape(TOK_DEV, HEAD_COUNT, DH)
        score_grad = round_bf(jnp.einsum('the,she->hts', grad_heads, value_f) * decay_mat)
        query_grad = jnp.einsum('hts,shd->thd', score_grad, key_f) + growth * jnp.einsum('the,hde->thd', grad_heads, states_bf)
        key_part = jnp.einsum('hts,thd->shd', score_grad, query_f)
        value_part = jnp.einsum('hts,the->she', weights, grad_heads)
        key_decayed = round_bf(key_f * shrink)
        summary = jnp.einsum('shd,she->hde', key_decayed, value_f)
        query_decayed = round_bf(query_f * growth)
        grad_summary = jnp.einsum('thd,the->hde', query_decayed, grad_heads)
        states_next = jnp.exp(block_log)[:, None, None] * states_prev + summary
        return (states_next, (query_grad.astype(jnp.bfloat16), key_part, value_part, grad_summary, block_log))
    unused_state, per_block = lax.scan(forward_step, state_in, (query_blocks, key_blocks, value_blocks, grad_blocks, decay_blocks))
    query_grads, key_parts, value_parts, grad_summaries, block_logs = per_block

    def reverse_step(grads_here, inputs):
        summary_here, log_here = inputs
        return (summary_here + jnp.exp(log_here)[:, None, None] * grads_here, grads_here)
    final_carry, grads_all = lax.scan(reverse_step, state_out_grad, (grad_summaries, block_logs), reverse=True)

    def finish_step(inputs):
        key_heads, value_heads, decay_rows, key_part, value_part, grads_here = inputs
        cum_log = jnp.cumsum(decay_rows, axis=1)
        block_log = cum_log[:, -1]
        shrink = jnp.exp(block_log[:, None] - cum_log).T[:, :, None]
        grads_bf = round_bf(grads_here)
        key_f = key_heads.astype(jnp.float32)
        value_f = value_heads.astype(jnp.float32)
        key_grad = key_part + shrink * jnp.einsum('hde,she->shd', grads_bf, value_f)
        value_grad = value_part + shrink * jnp.einsum('hde,shd->she', grads_bf, key_f)
        return (key_grad.astype(jnp.bfloat16), value_grad.astype(jnp.bfloat16))
    key_grads, value_grads = lax.map(finish_step, (key_blocks, value_blocks, decay_blocks, key_parts, value_parts, grads_all))
    return (query_grads.reshape(SLAB_TOKENS, feature_count), key_grads.reshape(SLAB_TOKENS, feature_count), value_grads.reshape(SLAB_TOKENS, feature_count), final_carry)
```

```python
import jax
import jax.numpy as jnp
from jax import lax
from jax.experimental import pallas as pl
from jax.experimental.pallas import tpu as pltpu
from jax.sharding import PartitionSpec as P

EPSILON = 1e-06
MESH = pl.DeviceIdType.MESH
F32 = jnp.float32
BF16 = jnp.bfloat16

NX, NZ, NY = 4, 12, 8
CHIPS = NX * NZ
HL, TOK, DH = 4, 256, 128
TILES = 32
OWN_Z = 8


def far_first(step, count):
    return count // 2 + ((step + 1) // 2) * (1 - 2 * (step % 2))


def dot(a, b, dims):
    return lax.dot_general(a, b, (dims, ((), ())), preferred_element_type=F32)


NN = ((1,), (0,))
NT = ((1,), (1,))
TN = ((0,), (0,))


def kernel(
    q_hbm, k_hbm, v_hbm, ld_hbm, og_hbm, gain_hbm, sin_hbm, sout_hbm,
    qg_out, kg_out, vg_out, sg_out,
    q, k, v, og, gain, ld, tile_in, tile_out,
    cum_pad, cum_col, bl_mine, bl_other, dec_src, dec_all,
    sum_send, sum_recv, rows_pad, cols_pad,
    summ, summ_recv, t_src, t_all, p_src, p_ret, p_fwd, p_other,
    gsum, gsum_recv, u_src, u_all, h_src, h_ret, h_fwd, h_other, g_src, g_all,
    states_bf, grads_bf, dmat, wts, growth, shrink, attended, gained, qdec, agrad,
    kpart, vpart, qg, kg, vg,
    in_sem, x_send, x_recv, a_send, a_recv, out_sem,
):
    s = lax.axis_index("seq")
    y = lax.axis_index("head")
    c = s % 2
    p = s // 2
    x = p // NZ
    z = p % NZ
    is_owner = z % 3 != 2
    zi = (z // 3) * 2 + jnp.minimum(z % 3, 1)
    my_tile = x * OWN_Z + zi
    partner = (s + 1 - 2 * c, y)
    mine, theirs = 2 * c, 2 - 2 * c

    loads = {}

    def load(name, slot, src, dst):
        copy = pltpu.make_async_copy(src, dst, in_sem.at[slot])
        copy.start()
        loads.setdefault(name, []).append(copy)

    def arrived(name):
        for copy in loads[name]:
            copy.wait()

    load("ld", 0, ld_hbm, ld)
    for index, (name, src, dst) in enumerate((("k", k_hbm, k), ("v", v_hbm, v), ("q", q_hbm, q), ("og", og_hbm, og))):
        for h in range(HL):
            load(name, 1 + index * HL + h, src.at[:, pl.ds(h * DH, DH)], dst.at[h])
    load("gain", 17, gain_hbm, gain)
    load("tile", 18, sin_hbm.at[c * TILES + my_tile], tile_in)
    load("tile", 19, sout_hbm.at[c * TILES + my_tile], tile_out)

    def chip_at(step):
        dx = far_first(step % NX, NX)
        dz = far_first(step // NX, NZ)
        return ((x + dx) % NX) * NZ + (z + dz) % NZ

    barrier = pltpu.get_barrier_semaphore()

    def greet_chip(step, carry):
        pl.semaphore_signal(barrier, inc=1, device_id=(chip_at(step) * 2 + c, y), device_id_type=MESH)
        return carry

    lax.fori_loop(0, CHIPS - 1, greet_chip, 0)

    def greet_head(step, carry):
        pl.semaphore_signal(barrier, inc=1, device_id=(s, (y + 1 + step) % NY), device_id_type=MESH)
        return carry

    lax.fori_loop(0, NY - 1, greet_head, 0)
    pl.semaphore_signal(barrier, inc=1, device_id=partner, device_id_type=MESH)

    cum_pad[...] = jnp.zeros_like(cum_pad)
    arrived("ld")
    cum_pad[0:HL, :] = ld[...]
    cum = cum_pad[0:8, :]
    lane = lax.broadcasted_iota(jnp.int32, (8, TOK), 1)
    for shift in (1, 2, 4, 8, 16, 32, 64, 128):
        cum = cum + jnp.where(lane >= shift, pltpu.roll(cum, shift, 1), 0.0)
    cum_pad[0:8, :] = cum
    cum_col[...] = cum_pad[...].T
    bl = jnp.broadcast_to(cum[:, TOK - 1 : TOK], (8, DH))
    bl_mine[...] = bl

    pl.semaphore_wait(barrier, CHIPS - 1 + NY)

    def swap(slot, src, dst):
        copy = pltpu.make_async_remote_copy(
            src_ref=src, dst_ref=dst, send_sem=x_send.at[slot], recv_sem=x_recv.at[slot],
            device_id=partner, device_id_type=MESH,
        )
        copy.start()
        return copy

    swap_bl = swap(0, bl_mine, bl_other)

    arrived("k")
    arrived("v")
    for h in range(HL):
        fade = jnp.exp(cum_col[TOK - 1 : TOK, h : h + 1] - cum_col[:, h : h + 1])
        shrink[h] = jnp.broadcast_to(fade, (TOK, DH))
        key_decayed = (k[h].astype(F32) * shrink[h]).astype(BF16)
        summ[h] = dot(key_decayed, v[h], TN)
    swap_summ = swap(1, summ.at[pl.ds(theirs, 2)], summ_recv)

    def to_owners(src_of, dst, slot, keep):
        def send(step):
            xt = (x + far_first(step % NX, NX)) % NX
            zt = (zi + far_first(step // NX, OWN_Z)) % OWN_Z
            tile = xt * OWN_Z + zt
            chip = xt * NZ + (zt // 2) * 3 + zt % 2
            pltpu.make_async_remote_copy(
                src_ref=src_of(tile), dst_ref=dst.at[p], send_sem=a_send.at[slot], recv_sem=a_recv.at[slot],
                device_id=(chip * 2 + c, y), device_id_type=MESH,
            ).start()

        def body(step, carry):
            send(step)
            return carry

        lax.fori_loop(0, TILES - 1, body, 0)

        @pl.when(jnp.logical_not(is_owner))
        def _():
            send(TILES - 1)

        @pl.when(is_owner)
        def _():
            dst[p] = keep()

    def from_owner(src_of, dst, slot):
        def body(step, carry):
            chip = chip_at(step)
            pltpu.make_async_remote_copy(
                src_ref=src_of(chip), dst_ref=dst.at[c, my_tile], send_sem=a_send.at[slot], recv_sem=a_recv.at[slot],
                device_id=(chip * 2 + c, y), device_id_type=MESH,
            ).start()
            return carry

        lax.fori_loop(0, CHIPS - 1, body, 0)

    def drain(sem, ref, count):
        window = ref.at[pl.ds(0, count)]
        pltpu.make_async_copy(window, window, sem).wait()

    def drain_tiles(sem, ref):
        @pl.when(is_owner)
        def _():
            drain(sem, ref, TILES - 1)

        @pl.when(jnp.logical_not(is_owner))
        def _():
            drain(sem, ref, TILES)

    swap_bl.wait_recv()
    e_mine = jnp.exp(bl_mine[...])
    e_other = jnp.exp(bl_other[...])
    e_chip = jnp.exp(bl_mine[...] + bl_other[...])
    for h in range(HL):
        dec_src[h] = jnp.broadcast_to(e_chip[h : h + 1, :], (8, DH))
    to_owners(
        lambda tile: dec_src.at[mine + tile // 16], dec_all, 0, lambda: dec_src[mine + my_tile // 16]
    )

    first = c == 0

    def pick_rows(value):
        return [jnp.where(first, value[i : i + 1, :], value[2 + i : 3 + i, :]) for i in range(2)]

    e_first = jnp.where(first, e_mine, e_other)
    e_second = jnp.where(first, e_other, e_mine)
    e_first_rows, e_second_rows = pick_rows(e_first), pick_rows(e_second)

    swap_summ.wait_recv()
    for i in range(2):
        own, other = summ[mine + i], summ_recv[i]
        early = jnp.where(first, own, other)
        late = jnp.where(first, other, own)
        t_src[16 * i : 16 * i + 16] = (e_second_rows[i] * early + late).reshape(16, 8, DH)
    to_owners(lambda tile: t_src.at[tile], t_all, 1, lambda: t_src[my_tile])

    arrived("q")
    row_id = lax.broadcasted_iota(jnp.int32, (TOK, TOK), 0)
    col_id = lax.broadcasted_iota(jnp.int32, (TOK, TOK), 1)
    for h in range(HL):
        col = cum_col[:, h : h + 1]
        spread = col - cum_pad[h : h + 1, :]
        decay = jnp.where(row_id >= col_id, jnp.exp(jnp.minimum(spread, 0.0)), 0.0)
        dmat[h] = decay
        weights = (dot(q[h], k[h], NT) * decay).astype(BF16)
        wts[h] = weights
        attended[h] = dot(weights, v[h], NN)
        growth[h] = jnp.broadcast_to(jnp.exp(col), (TOK, DH))
        qdec[h] = (q[h].astype(F32) * growth[h]).astype(BF16)

    arrived("tile")

    @pl.when(is_owner)
    def _():
        drain(a_recv.at[0], dec_all, CHIPS - 1)
        drain(a_recv.at[1], t_all, CHIPS - 1)

        def body(chip, state):
            p_src[chip] = state
            return dec_all[chip] * state + t_all[chip]

        lax.fori_loop(0, CHIPS, body, tile_in[...], unroll=4)
        from_owner(lambda chip: p_src.at[chip], p_ret, 2)
        p_ret[c, my_tile] = p_src[p]

    arrived("og")
    arrived("gain")
    for h in range(HL):
        gained[h] = gain[:, h * DH : (h + 1) * DH] * og[h].astype(F32)

    drain_tiles(a_recv.at[2], p_ret.at[c])
    for i in range(2):
        chip_state = p_ret[c, 16 * i : 16 * i + 16].reshape(DH, DH)
        after = e_first_rows[i] * chip_state + jnp.where(first, summ[mine + i], summ_recv[i])
        p_fwd[i] = jnp.where(first, after, chip_state)
        states_bf[mine + i] = jnp.where(first, chip_state, after).astype(BF16)
    swap_state = swap(2, p_fwd, p_other)

    def attend(h, square, inner):
        state_part = dot(q[h], states_bf[h], NN)
        out = attended[h] + growth[h] * state_part
        attended[h] = out
        return square + out * out, inner + gained[h] * out

    square = jnp.zeros((TOK, DH), F32)
    inner = jnp.zeros((TOK, DH), F32)
    for i in range(2):
        square, inner = attend(mine + i, square, inner)
    swap_state.wait_recv()
    for i in range(2):
        states_bf[theirs + i] = p_other[i].astype(BF16)
    for i in range(2):
        square, inner = attend(theirs + i, square, inner)

    sum_send[0:1, :] = jnp.sum(square.T, axis=0, keepdims=True)
    sum_send[1:2, :] = jnp.sum(inner.T, axis=0, keepdims=True)

    def send_sums(step, carry):
        pltpu.make_async_remote_copy(
            src_ref=sum_send, dst_ref=sum_recv.at[y], send_sem=a_send.at[3], recv_sem=a_recv.at[3],
            device_id=(s, (y + far_first(step, NY)) % NY), device_id_type=MESH,
        ).start()
        return carry

    lax.fori_loop(0, NY - 1, send_sums, 0)
    sum_recv[y] = sum_send[...]
    rows_pad[...] = jnp.zeros_like(rows_pad)
    drain(a_recv.at[3], sum_recv, NY - 1)
    total = sum_recv[0]
    for i in range(1, NY):
        total = total + sum_recv[i]
    features = HL * DH * NY
    inv_rms = lax.rsqrt(total[0:1, :] / features + EPSILON)
    rows_pad[0:1, :] = inv_rms
    rows_pad[1:2, :] = total[1:2, :] * (inv_rms * inv_rms * inv_rms) / features
    cols_pad[...] = rows_pad[...].T
    inv_col = cols_pad[:, 0:1]
    coef_col = cols_pad[:, 1:2]

    for h in range(HL):
        grad = (gained[h] * inv_col - attended[h] * coef_col).astype(BF16)
        agrad[h] = grad
        gsum[h] = dot(qdec[h], grad, TN)
    swap_grad = swap(3, gsum.at[pl.ds(theirs, 2)], gsum_recv)

    def score_part(h):
        score = (dot(agrad[h], v[h], NT) * dmat[h]).astype(BF16)
        query_grad = dot(score, k[h], NN) + growth[h] * dot(agrad[h], states_bf[h], NT)
        qg[h] = query_grad.astype(BF16)
        kpart[h] = dot(score, q[h], TN)
        vpart[h] = dot(wts[h], agrad[h], TN)

    swap_grad.wait_recv()
    for i in range(2):
        own, other = gsum[mine + i], gsum_recv[i]
        early = jnp.where(first, own, other)
        late = jnp.where(first, other, own)
        u_src[16 * i : 16 * i + 16] = (e_first_rows[i] * late + early).reshape(16, 8, DH)
    to_owners(lambda tile: u_src.at[tile], u_all, 4, lambda: u_src[my_tile])

    stores = []

    def store(slot, src, dst):
        copy = pltpu.make_async_copy(src, dst, out_sem.at[slot])
        copy.start()
        stores.append(copy)

    for h in range(HL):
        score_part(h)
        store(h, qg.at[h], qg_out.at[:, pl.ds(h * DH, DH)])

    @pl.when(is_owner)
    def _():
        drain(a_recv.at[4], u_all, CHIPS - 1)

        def body(step, grad):
            chip = CHIPS - 1 - step
            h_src[chip] = grad
            return dec_all[chip] * grad + u_all[chip]

        g_src[...] = lax.fori_loop(0, CHIPS, body, tile_out[...], unroll=4)
        from_owner(lambda chip: h_src.at[chip], h_ret, 5)
        h_ret[c, my_tile] = h_src[p]
        from_owner(lambda chip: g_src, g_all, 6)
        g_all[c, my_tile] = g_src[...]

    drain_tiles(a_recv.at[5], h_ret.at[c])
    for i in range(2):
        chip_grad = h_ret[c, 16 * i : 16 * i + 16].reshape(DH, DH)
        before = e_second_rows[i] * chip_grad + jnp.where(first, gsum_recv[i], gsum[mine + i])
        h_fwd[i] = jnp.where(first, chip_grad, before)
        grads_bf[mine + i] = jnp.where(first, before, chip_grad).astype(BF16)
    swap_back = swap(4, h_fwd, h_other)

    def finish(h):
        key_grad = kpart[h] + shrink[h] * dot(v[h], grads_bf[h], NT)
        kg[h] = key_grad.astype(BF16)
        value_grad = vpart[h] + shrink[h] * dot(k[h], grads_bf[h], NN)
        vg[h] = value_grad.astype(BF16)

    for i in range(2):
        finish(mine + i)
    swap_back.wait_recv()
    for i in range(2):
        grads_bf[theirs + i] = h_other[i].astype(BF16)
    for i in range(2):
        finish(theirs + i)
    for h in range(HL):
        store(HL + h, kg.at[h], kg_out.at[:, pl.ds(h * DH, DH)])
        store(2 * HL + h, vg.at[h], vg_out.at[:, pl.ds(h * DH, DH)])

    drain_tiles(a_recv.at[6], g_all.at[c])
    swap_slab = swap(5, g_all.at[c], g_all.at[c])
    store(3 * HL, g_all.at[c], sg_out.at[c])
    swap_slab.wait_recv()
    store(3 * HL + 1, g_all.at[1 - c], sg_out.at[1 - c])

    for copy in (swap_bl, swap_summ, swap_state, swap_grad, swap_back, swap_slab):
        copy.wait_send()
    for slot, ref in ((0, t_src), (1, t_src), (4, u_src)):
        drain_tiles(a_send.at[slot], ref)
    drain(a_send.at[3], sum_recv, NY - 1)

    @pl.when(is_owner)
    def _():
        for slot in (2, 5, 6):
            drain(a_send.at[slot], p_src, CHIPS - 1)

    for copy in stores:
        copy.wait()


def on_device(query_rows, key_rows, value_rows, log_decay, out_grad, norm_gain, state_in, state_out_grad):
    any_space = pl.BlockSpec(memory_space=pl.ANY)

    def vm(*shape, dtype=F32):
        return pltpu.VMEM(shape, dtype)

    tiles = vm(TILES, 8, DH)
    landing = vm(CHIPS, 8, DH)
    halves = vm(2, TILES, 8, DH)
    pair = vm(2, DH, DH)
    heads = vm(HL, TOK, DH)
    heads_bf = vm(HL, TOK, DH, dtype=BF16)
    state = vm(HL, DH, DH)
    state_bf = vm(HL, DH, DH, dtype=BF16)
    dma = pltpu.SemaphoreType.DMA
    rows = jax.ShapeDtypeStruct(query_rows.shape, BF16)
    slab = jax.ShapeDtypeStruct((2, TILES, 8, DH), F32)
    qg, kg, vg, sg = pl.pallas_call(
        kernel,
        out_shape=(rows, rows, rows, slab),
        in_specs=[any_space] * 8,
        out_specs=(any_space,) * 4,
        scratch_shapes=[
            heads_bf, heads_bf, heads_bf, heads_bf, vm(1, HL * DH), vm(HL, TOK), vm(8, DH), vm(8, DH),
            vm(DH, TOK), vm(TOK, DH), vm(8, DH), vm(8, DH), vm(HL, 8, DH), landing,
            vm(2, TOK), vm(NY, 2, TOK), vm(DH, TOK), vm(TOK, DH),
            state, pair, tiles, landing, landing, halves, pair, pair,
            state, pair, tiles, landing, landing, halves, pair, pair, vm(8, DH), halves,
            state_bf, state_bf, vm(HL, TOK, TOK), vm(HL, TOK, TOK, dtype=BF16), heads, heads, heads, heads, heads_bf, heads_bf,
            heads, heads, heads_bf, heads_bf, heads_bf,
            dma((20,)), dma((6,)), dma((6,)), dma((7,)), dma((7,)), dma((3 * HL + 2,)),
        ],
        compiler_params=pltpu.CompilerParams(
            collective_id=0, has_side_effects=True, vmem_limit_bytes=48 * 1024 * 1024
        ),
    )(
        query_rows, key_rows, value_rows, log_decay, out_grad, norm_gain.reshape(1, HL * DH),
        state_in.reshape(2 * TILES, 8, DH), state_out_grad.reshape(2 * TILES, 8, DH),
    )
    return qg, kg, vg, sg.reshape(HL, DH, DH)


def solution(mesh):
    wide = P("seq", "head")
    state = P("head", None, None)
    return jax.shard_map(
        on_device,
        mesh=mesh,
        in_specs=(wide, wide, wide, P("head", "seq"), wide, P("head"), state, state),
        out_specs=(wide, wide, wide, state),
        check_vma=False,
    )
```

```python
import jax
import jax.numpy as jnp
from jax import lax
from jax.experimental import pallas as pl
from jax.experimental.pallas import tpu as pltpu
from jax.sharding import PartitionSpec as P

EPSILON = 1e-06
MESH = pl.DeviceIdType.MESH
F32 = jnp.float32
BF16 = jnp.bfloat16

NX, NZ, NY = 4, 12, 8
CHIPS = NX * NZ
HL, TOK, DH = 4, 256, 128
TILES = 32
OWN_Z = 8
X_STEPS = (2, 1, 3, 0)
Y_STEPS = (4, 3, 5, 2, 6, 1, 7)


def far_first(step, count):
    return count // 2 + ((step + 1) >> 1) * (1 - 2 * (step & 1))


def dot(a, b, dims):
    return lax.dot_general(a, b, (dims, ((), ())), preferred_element_type=F32)


NN = ((1,), (0,))
NT = ((1,), (1,))
TN = ((0,), (0,))


def at_least(value, bounds):
    return sum((value >= bound).astype(jnp.int32) for bound in bounds)


def kernel(
    q_hbm, k_hbm, v_hbm, ld_hbm, og_hbm, gain_hbm, sin_hbm, sout_hbm,
    qg, kg, vg, sg,
    q, k, v, og, gain, ld, tile_in, tile_out,
    cum_pad, cum_col, bl_mine, bl_other, dec_src, dec_all,
    sum_send, sum_recv, rows_pad, cols_pad,
    summ, summ_recv, t_src, t_all, p_src, p_ret, p_fwd, p_other,
    gsum, gsum_recv, u_src, u_all, h_src, h_ret, h_fwd, h_other, g_src, g_all,
    states_bf, grads_bf, dmat, wts, growth, shrink, attended, gained, qdec, agrad,
    kpart, vpart,
    in_sem, x_send, x_recv, a_send, a_recv,
):
    s = lax.axis_index("seq")
    y = lax.axis_index("head")
    c = s & 1
    p = s >> 1
    x = at_least(p, (NZ, 2 * NZ, 3 * NZ))
    z = p - NZ * x
    third = at_least(z, (3, 6, 9))
    z_rest = z - 3 * third
    is_owner = z_rest != 2
    zi = 2 * third + jnp.minimum(z_rest, 1)
    my_tile = x * OWN_Z + zi
    partner = (s + 1 - 2 * c, y)
    mine, theirs = 2 * c, 2 - 2 * c
    xs = {dx: (x + dx) & (NX - 1) for dx in X_STEPS}

    def load(slot, *pairs):
        for src, dst in pairs:
            pltpu.make_async_copy(src, dst, in_sem.at[slot]).start()

    def arrived(slot, dst):
        pltpu.make_async_copy(dst, dst, in_sem.at[slot]).wait()

    def load_heads(slot, src, dst):
        load(slot, *((src.at[:, pl.ds(h * DH, DH)], dst.at[h]) for h in range(HL)))

    load(0, (ld_hbm, ld))
    load_heads(1, k_hbm, k)
    load_heads(2, v_hbm, v)
    load_heads(3, q_hbm, q)
    load_heads(4, og_hbm, og)
    load(5, (gain_hbm, gain))
    load(6, (sin_hbm.at[c * TILES + my_tile], tile_in))
    load(7, (sout_hbm.at[c * TILES + my_tile], tile_out))

    def to_chips(send):
        def ring(step, steps):
            zt = z + far_first(step, NZ)
            zt = jnp.where(zt >= NZ, zt - NZ, zt)
            for dx in steps:
                send(xs[dx] * NZ + zt)

        def body(step, carry):
            ring(step, X_STEPS)
            return carry

        lax.fori_loop(0, NZ - 1, body, 0)
        ring(NZ - 1, X_STEPS[:-1])

    barrier = pltpu.get_barrier_semaphore()

    def greet(s_there, y_there):
        pl.semaphore_signal(barrier, inc=1, device_id=(s_there, y_there), device_id_type=MESH)

    to_chips(lambda chip: greet(chip * 2 + c, y))
    for dy in Y_STEPS:
        greet(s, (y + dy) & (NY - 1))
    greet(*partner)

    cum_pad[...] = jnp.zeros_like(cum_pad)
    arrived(0, ld)
    cum_pad[0:HL, :] = ld[...]
    cum = cum_pad[0:8, :]
    lane = lax.broadcasted_iota(jnp.int32, (8, TOK), 1)
    for shift in (1, 2, 4, 8, 16, 32, 64, 128):
        cum = cum + jnp.where(lane >= shift, pltpu.roll(cum, shift, 1), 0.0)
    cum_pad[0:8, :] = cum
    cum_col[...] = cum_pad[...].T
    bl = jnp.broadcast_to(cum[:, TOK - 1 : TOK], (8, DH))
    bl_mine[...] = bl

    arrived(1, k)
    arrived(2, v)
    for h in range(HL):
        fade = jnp.exp(cum_col[TOK - 1 : TOK, h : h + 1] - cum_col[:, h : h + 1])
        shrink[h] = jnp.broadcast_to(fade, (TOK, DH))
        key_decayed = (k[h].astype(F32) * shrink[h]).astype(BF16)
        summ[h] = dot(key_decayed, v[h], TN)

    pl.semaphore_wait(barrier, CHIPS - 1 + NY)

    def swap(slot, src, dst):
        copy = pltpu.make_async_remote_copy(
            src_ref=src, dst_ref=dst, send_sem=x_send.at[slot], recv_sem=x_recv.at[slot],
            device_id=partner, device_id_type=MESH,
        )
        copy.start()
        return copy

    swap_bl = swap(0, bl_mine, bl_other)
    swap_summ = swap(1, summ.at[pl.ds(theirs, 2)], summ_recv)

    def push(src, dst, slot, s_there, y_there):
        pltpu.make_async_remote_copy(
            src_ref=src, dst_ref=dst, send_sem=a_send.at[slot], recv_sem=a_recv.at[slot],
            device_id=(s_there, y_there), device_id_type=MESH,
        ).start()

    def to_owners(src_of, dst, slot, keep):
        def ring(step, steps):
            zt = (zi + far_first(step, OWN_Z)) & (OWN_Z - 1)
            z_there = (zt >> 1) * 3 + (zt & 1)
            for dx in steps:
                push(src_of(xs[dx] * OWN_Z + zt), dst.at[p], slot, (xs[dx] * NZ + z_there) * 2 + c, y)

        def body(step, carry):
            ring(step, X_STEPS)
            return carry

        lax.fori_loop(0, OWN_Z - 1, body, 0)
        ring(OWN_Z - 1, X_STEPS[:-1])

        @pl.when(jnp.logical_not(is_owner))
        def _():
            ring(OWN_Z - 1, X_STEPS[-1:])

        @pl.when(is_owner)
        def _():
            dst[p] = keep()

    def drain(sem, ref, count):
        window = ref.at[pl.ds(0, count)]
        pltpu.make_async_copy(window, window, sem).wait()

    def drain_tiles(sem, ref, count=TILES):
        @pl.when(is_owner)
        def _():
            drain(sem, ref, count - 1)

        @pl.when(jnp.logical_not(is_owner))
        def _():
            drain(sem, ref, count)

    swap_bl.wait_recv()
    e_mine = jnp.exp(bl_mine[...])
    e_other = jnp.exp(bl_other[...])
    e_chip = jnp.exp(bl_mine[...] + bl_other[...])
    for h in range(HL):
        dec_src[h] = e_chip[h : h + 1, :]
    to_owners(
        lambda tile: dec_src.at[mine + tile // 16], dec_all, 0, lambda: dec_src[mine + my_tile // 16]
    )

    first = c == 0

    def pick_rows(value):
        return [jnp.where(first, value[i : i + 1, :], value[2 + i : 3 + i, :]) for i in range(2)]

    e_first = jnp.where(first, e_mine, e_other)
    e_second = jnp.where(first, e_other, e_mine)
    e_first_rows, e_second_rows = pick_rows(e_first), pick_rows(e_second)

    swap_summ.wait_recv()
    for i in range(2):
        own, other = summ[mine + i], summ_recv[i]
        early = jnp.where(first, own, other)
        late = jnp.where(first, other, own)
        t_src[16 * i : 16 * i + 16] = (e_second_rows[i] * early + late).reshape(16, 8, DH)
    to_owners(lambda tile: t_src.at[tile], t_all, 1, lambda: t_src[my_tile])

    arrived(3, q)
    row_id = lax.broadcasted_iota(jnp.int32, (TOK, TOK), 0)
    col_id = lax.broadcasted_iota(jnp.int32, (TOK, TOK), 1)
    for h in range(HL):
        col = cum_col[:, h : h + 1]
        spread = col - cum_pad[h : h + 1, :]
        decay = jnp.where(row_id >= col_id, jnp.exp(jnp.minimum(spread, 0.0)), 0.0)
        dmat[h] = decay
        weights = (dot(q[h], k[h], NT) * decay).astype(BF16)
        wts[h] = weights
        attended[h] = dot(weights, v[h], NN)
        growth[h] = jnp.broadcast_to(jnp.exp(col), (TOK, DH))
        qdec[h] = (q[h].astype(F32) * growth[h]).astype(BF16)

    arrived(6, tile_in)
    arrived(7, tile_out)

    @pl.when(is_owner)
    def _():
        drain(a_recv.at[0], dec_all, CHIPS - 1)
        drain(a_recv.at[1], t_all, CHIPS - 1)

        def body(chip, state):
            p_src[chip] = state
            return dec_all[chip] * state + t_all[chip]

        lax.fori_loop(0, CHIPS, body, tile_in[...], unroll=4)
        to_chips(lambda chip: push(p_src.at[chip], p_ret.at[c, my_tile], 2, chip * 2 + c, y))
        p_ret[c, my_tile] = p_src[p]

    arrived(4, og)
    arrived(5, gain)
    for h in range(HL):
        gained[h] = gain[:, h * DH : (h + 1) * DH] * og[h].astype(F32)

    drain_tiles(a_recv.at[2], p_ret.at[c])
    for i in range(2):
        chip_state = p_ret[c, 16 * i : 16 * i + 16].reshape(DH, DH)
        after = e_first_rows[i] * chip_state + jnp.where(first, summ[mine + i], summ_recv[i])
        p_fwd[i] = jnp.where(first, after, chip_state)
        states_bf[mine + i] = jnp.where(first, chip_state, after).astype(BF16)
    swap_state = swap(2, p_fwd, p_other)

    def attend(h, square, inner):
        state_part = dot(q[h], states_bf[h], NN)
        out = attended[h] + growth[h] * state_part
        attended[h] = out
        return square + out * out, inner + gained[h] * out

    square = jnp.zeros((TOK, DH), F32)
    inner = jnp.zeros((TOK, DH), F32)
    for i in range(2):
        square, inner = attend(mine + i, square, inner)
    swap_state.wait_recv()
    for i in range(2):
        states_bf[theirs + i] = p_other[i].astype(BF16)
    for i in range(2):
        square, inner = attend(theirs + i, square, inner)

    sum_send[0:1, :] = jnp.sum(square.T, axis=0, keepdims=True)
    sum_send[1:2, :] = jnp.sum(inner.T, axis=0, keepdims=True)

    for dy in Y_STEPS:
        push(sum_send, sum_recv.at[y], 3, s, (y + dy) & (NY - 1))
    sum_recv[y] = sum_send[...]
    rows_pad[...] = jnp.zeros_like(rows_pad)
    drain(a_recv.at[3], sum_recv, NY - 1)
    total = sum_recv[0]
    for i in range(1, NY):
        total = total + sum_recv[i]
    features = HL * DH * NY
    inv_rms = lax.rsqrt(total[0:1, :] / features + EPSILON)
    rows_pad[0:1, :] = inv_rms
    rows_pad[1:2, :] = total[1:2, :] * (inv_rms * inv_rms * inv_rms) / features
    cols_pad[...] = rows_pad[...].T
    inv_col = cols_pad[:, 0:1]
    coef_col = cols_pad[:, 1:2]

    for h in range(HL):
        grad = (gained[h] * inv_col - attended[h] * coef_col).astype(BF16)
        agrad[h] = grad
        gsum[h] = dot(qdec[h], grad, TN)
    swap_grad = swap(3, gsum.at[pl.ds(theirs, 2)], gsum_recv)

    def score_part(h):
        score = (dot(agrad[h], v[h], NT) * dmat[h]).astype(BF16)
        query_grad = dot(score, k[h], NN) + growth[h] * dot(agrad[h], states_bf[h], NT)
        qg[h] = query_grad.astype(BF16)
        kpart[h] = dot(score, q[h], TN)
        vpart[h] = dot(wts[h], agrad[h], TN)

    swap_grad.wait_recv()
    for i in range(2):
        own, other = gsum[mine + i], gsum_recv[i]
        early = jnp.where(first, own, other)
        late = jnp.where(first, other, own)
        u_src[16 * i : 16 * i + 16] = (e_first_rows[i] * late + early).reshape(16, 8, DH)
    to_owners(lambda tile: u_src.at[tile], u_all, 4, lambda: u_src[my_tile])

    for h in range(HL):
        score_part(h)

    @pl.when(is_owner)
    def _():
        drain(a_recv.at[4], u_all, CHIPS - 1)

        def body(step, grad):
            chip = CHIPS - 1 - step
            h_src[chip] = grad
            return dec_all[chip] * grad + u_all[chip]

        g_src[...] = lax.fori_loop(0, CHIPS, body, tile_out[...], unroll=4)
        for dz in (6, 5, 7, 4, 8, 3, 9, 2, 10, 1, 11):
            zt = z + dz
            zt = jnp.where(zt >= NZ, zt - NZ, zt)
            push(g_src, g_all.at[c, my_tile], 6, (x * NZ + zt) * 2 + c, y)
        to_chips(lambda chip: push(h_src.at[chip], h_ret.at[c, my_tile], 5, chip * 2 + c, y))
        h_ret[c, my_tile] = h_src[p]
        g_all[c, my_tile] = g_src[...]

    drain_tiles(a_recv.at[6], g_all.at[c], OWN_Z)
    line = g_all.at[c, pl.ds(x * OWN_Z, OWN_Z)]
    for dx in X_STEPS[:-1]:
        push(line, line, 7, (xs[dx] * NZ + z) * 2 + c, y)

    drain_tiles(a_recv.at[5], h_ret.at[c])
    for i in range(2):
        chip_grad = h_ret[c, 16 * i : 16 * i + 16].reshape(DH, DH)
        before = e_second_rows[i] * chip_grad + jnp.where(first, gsum_recv[i], gsum[mine + i])
        h_fwd[i] = jnp.where(first, chip_grad, before)
        grads_bf[mine + i] = jnp.where(first, before, chip_grad).astype(BF16)
    swap_back = swap(4, h_fwd, h_other)

    def finish(h):
        key_grad = kpart[h] + shrink[h] * dot(v[h], grads_bf[h], NT)
        kg[h] = key_grad.astype(BF16)
        value_grad = vpart[h] + shrink[h] * dot(k[h], grads_bf[h], NN)
        vg[h] = value_grad.astype(BF16)

    for i in range(2):
        finish(mine + i)
    swap_back.wait_recv()
    for i in range(2):
        grads_bf[theirs + i] = h_other[i].astype(BF16)
    for i in range(2):
        finish(theirs + i)

    drain(a_recv.at[7], g_all.at[c], TILES - OWN_Z)
    swap_slab = swap(5, g_all.at[c], g_all.at[c])
    swap_slab.wait_recv()
    sg[...] = g_all[...]

    for copy in (swap_bl, swap_summ, swap_state, swap_grad, swap_back, swap_slab):
        copy.wait_send()
    for slot, ref in ((0, dec_all), (1, t_src), (4, u_src)):
        drain_tiles(a_send.at[slot], ref)
    drain(a_send.at[3], sum_recv, NY - 1)

    @pl.when(is_owner)
    def _():
        for slot in (2, 5):
            drain(a_send.at[slot], p_src, CHIPS - 1)
        drain(a_send.at[6], p_src, NZ - 1)

    drain(a_send.at[7], p_src, TILES - OWN_Z)


def store_kernel(qg, kg, vg, sg, qg_out, kg_out, vg_out, sg_out, sem):
    copies = [pltpu.make_async_copy(sg, sg_out, sem.at[3 * HL])]
    for index, (src, dst) in enumerate(((qg, qg_out), (kg, kg_out), (vg, vg_out))):
        for h in range(HL):
            copies.append(pltpu.make_async_copy(src.at[h], dst.at[:, pl.ds(h * DH, DH)], sem.at[index * HL + h]))
    for copy in copies:
        copy.start()
    for copy in copies:
        copy.wait()


def on_device(query_rows, key_rows, value_rows, log_decay, out_grad, norm_gain, state_in, state_out_grad):
    hbm = pl.BlockSpec(memory_space=pltpu.HBM)
    vmem = pl.BlockSpec(memory_space=pltpu.VMEM)

    def vm(*shape, dtype=F32):
        return pltpu.VMEM(shape, dtype)

    tiles = vm(TILES, 8, DH)
    landing = vm(CHIPS, 8, DH)
    halves = vm(2, TILES, 8, DH)
    pair = vm(2, DH, DH)
    heads = vm(HL, TOK, DH)
    heads_bf = vm(HL, TOK, DH, dtype=BF16)
    state = vm(HL, DH, DH)
    state_bf = vm(HL, DH, DH, dtype=BF16)
    dma = pltpu.SemaphoreType.DMA
    rows = jax.ShapeDtypeStruct(query_rows.shape, BF16)
    slab = jax.ShapeDtypeStruct((2, TILES, 8, DH), F32)
    by_head = vm(HL, TOK, DH, dtype=BF16)
    arrays = (
        query_rows, key_rows, value_rows, log_decay, out_grad, norm_gain.reshape(1, HL * DH),
        state_in.reshape(2 * TILES, 8, DH), state_out_grad.reshape(2 * TILES, 8, DH),
    )
    grads = pl.pallas_call(
        kernel,
        out_shape=(by_head, by_head, by_head, vm(2, TILES, 8, DH)),
        in_specs=[hbm] * 8,
        out_specs=(vmem,) * 4,
        scratch_shapes=[
            heads_bf, heads_bf, heads_bf, heads_bf, vm(1, HL * DH), vm(HL, TOK), vm(8, DH), vm(8, DH),
            vm(DH, TOK), vm(TOK, DH), vm(8, DH), vm(8, DH), vm(HL, 1, DH), vm(CHIPS, 1, DH),
            vm(2, TOK), vm(NY, 2, TOK), vm(DH, TOK), vm(TOK, DH),
            state, pair, tiles, landing, landing, halves, pair, pair,
            state, pair, tiles, landing, landing, halves, pair, pair, vm(8, DH), halves,
            state_bf, state_bf, vm(HL, TOK, TOK), vm(HL, TOK, TOK, dtype=BF16), heads, heads, heads, heads, heads_bf, heads_bf,
            heads, heads,
            dma((8,)), dma((6,)), dma((6,)), dma((8,)), dma((8,)),
        ],
        compiler_params=pltpu.CompilerParams(
            collective_id=0, has_side_effects=True, vmem_limit_bytes=32 * 1024 * 1024
        ),
    )(*(pltpu.with_memory_space_constraint(array, pltpu.HBM) for array in arrays))
    qg, kg, vg, sg = pl.pallas_call(
        store_kernel,
        out_shape=(rows, rows, rows, slab),
        in_specs=[vmem] * 4,
        out_specs=(hbm,) * 4,
        scratch_shapes=[dma((3 * HL + 1,))],
        compiler_params=pltpu.CompilerParams(vmem_limit_bytes=4 * 1024 * 1024),
    )(*(pltpu.with_memory_space_constraint(grad, pltpu.VMEM) for grad in grads))
    return qg, kg, vg, sg.reshape(HL, DH, DH)


def solution(mesh):
    wide = P("seq", "head")
    state = P("head", None, None)
    return jax.shard_map(
        on_device,
        mesh=mesh,
        in_specs=(wide, wide, wide, P("head", "seq"), wide, P("head"), state, state),
        out_specs=(wide, wide, wide, state),
        check_vma=False,
    )
```

```python
import jax
import jax.numpy as jnp
from jax import lax
from jax.experimental import pallas as pl
from jax.experimental.pallas import tpu as pltpu
from jax.sharding import PartitionSpec as P

EPSILON = 1e-06
MESH = pl.DeviceIdType.MESH
F32 = jnp.float32
BF16 = jnp.bfloat16

NX, NZ, NY = 4, 12, 8
CHIPS = NX * NZ
HL, TOK, DH = 4, 256, 128
TILES = 32
OWN_Z = 8
X_STEPS = (2, 1, 3, 0)
Y_STEPS = (4, 3, 5, 2, 6, 1, 7)


def far_first(step, count):
    return count // 2 + ((step + 1) >> 1) * (1 - 2 * (step & 1))


def dot(a, b, dims):
    return lax.dot_general(a, b, (dims, ((), ())), preferred_element_type=F32)


NN = ((1,), (0,))
NT = ((1,), (1,))
TN = ((0,), (0,))


def at_least(value, bounds):
    return sum((value >= bound).astype(jnp.int32) for bound in bounds)


def kernel(
    q_hbm, k_hbm, v_hbm, ld_hbm, og_hbm, gain_hbm, sin_hbm, sout_hbm,
    qg, kg, vg, sg,
    q, k, v, og, gain, ld, tile_in, tile_out,
    cum_pad, cum_col, cum_recv, cum_two, cum_two_col, dec_src, dec_all,
    sum_send, sum_recv, rows_pad, cols_pad,
    summ, summ_recv, s_first, t_src, t_all, p_src, p_ret,
    gsum, u_src, u_all, h_src, h_ret, h_fwd, h_other, g_src, g_all,
    in_src, in_recv, q2, k2, v2, og2,
    states_bf, grads_bf, dmat, wts, growth, shrink, attended, gained, qdec, agrad,
    qpart, kpart, vpart, qpart_recv, kpart_recv, vpart_recv,
    in_sem, x_send, x_recv, a_send, a_recv,
):
    s = lax.axis_index("seq")
    y = lax.axis_index("head")
    c = s & 1
    p = s >> 1
    x = at_least(p, (NZ, 2 * NZ, 3 * NZ))
    z = p - NZ * x
    third = at_least(z, (3, 6, 9))
    z_rest = z - 3 * third
    is_owner = z_rest != 2
    zi = 2 * third + jnp.minimum(z_rest, 1)
    my_tile = x * OWN_Z + zi
    partner = (s + 1 - 2 * c, y)
    mine, theirs = 2 * c, 2 - 2 * c
    first = c == 0
    xs = {dx: (x + dx) & (NX - 1) for dx in X_STEPS}

    def load(slot, *pairs):
        for src, dst in pairs:
            pltpu.make_async_copy(src, dst, in_sem.at[slot]).start()

    def arrived(slot, dst):
        pltpu.make_async_copy(dst, dst, in_sem.at[slot]).wait()

    def load_heads(slot, src, dst):
        load(slot, *((src.at[:, pl.ds(h * DH, DH)], dst.at[h]) for h in range(HL)))

    load(0, (ld_hbm, ld))
    load_heads(1, k_hbm, k)
    load_heads(2, v_hbm, v)
    load_heads(3, q_hbm, q)
    load_heads(4, og_hbm, og)
    load(5, (gain_hbm, gain))
    load(6, (sin_hbm.at[c * TILES + my_tile], tile_in))
    load(7, (sout_hbm.at[c * TILES + my_tile], tile_out))

    def to_chips(send):
        def ring(step, steps):
            zt = z + far_first(step, NZ)
            zt = jnp.where(zt >= NZ, zt - NZ, zt)
            for dx in steps:
                send(xs[dx] * NZ + zt)

        def body(step, carry):
            ring(step, X_STEPS)
            return carry

        lax.fori_loop(0, NZ - 1, body, 0)
        ring(NZ - 1, X_STEPS[:-1])

    barrier = pltpu.get_barrier_semaphore()

    def greet(s_there, y_there):
        pl.semaphore_signal(barrier, inc=1, device_id=(s_there, y_there), device_id_type=MESH)

    to_chips(lambda chip: greet(chip * 2 + c, y))
    for dy in Y_STEPS:
        for core in range(2):
            greet(2 * p + core, (y + dy) & (NY - 1))
    greet(*partner)

    cum_pad[...] = jnp.zeros_like(cum_pad)
    arrived(0, ld)
    cum_pad[0:HL, :] = ld[...]
    cum = cum_pad[0:8, :]
    lane = lax.broadcasted_iota(jnp.int32, (8, TOK), 1)
    for shift in (1, 2, 4, 8, 16, 32, 64, 128):
        cum = cum + jnp.where(lane >= shift, pltpu.roll(cum, shift, 1), 0.0)
    cum_pad[0:8, :] = cum
    cum_col[...] = cum_pad[...].T

    arrived(1, k)
    arrived(2, v)
    for h in range(HL):
        fade = jnp.exp(cum_col[TOK - 1 : TOK, h : h + 1] - cum_col[:, h : h + 1])
        shrink[h] = jnp.broadcast_to(fade, (TOK, DH))
        key_decayed = (k[h].astype(F32) * shrink[h]).astype(BF16)
        summ[h] = dot(key_decayed, v[h], TN)

    pl.semaphore_wait(barrier, CHIPS - 1 + 2 * NY - 1)

    def swap(slot, src, dst):
        copy = pltpu.make_async_remote_copy(
            src_ref=src, dst_ref=dst, send_sem=x_send.at[slot], recv_sem=x_recv.at[slot],
            device_id=partner, device_id_type=MESH,
        )
        copy.start()
        return copy

    swap_cum = swap(0, cum_pad.at[pl.ds(0, 8)], cum_recv)
    swap_summ = swap(1, summ.at[pl.ds(theirs, 2)], summ_recv)

    def push(src, dst, slot, s_there, y_there):
        pltpu.make_async_remote_copy(
            src_ref=src, dst_ref=dst, send_sem=a_send.at[slot], recv_sem=a_recv.at[slot],
            device_id=(s_there, y_there), device_id_type=MESH,
        ).start()

    def to_owners(src_of, dst, slot, keep):
        def ring(step, steps):
            zt = (zi + far_first(step, OWN_Z)) & (OWN_Z - 1)
            z_there = (zt >> 1) * 3 + (zt & 1)
            for dx in steps:
                push(src_of(xs[dx] * OWN_Z + zt), dst.at[p], slot, (xs[dx] * NZ + z_there) * 2 + c, y)

        def body(step, carry):
            ring(step, X_STEPS)
            return carry

        lax.fori_loop(0, OWN_Z - 1, body, 0)
        ring(OWN_Z - 1, X_STEPS[:-1])

        @pl.when(jnp.logical_not(is_owner))
        def _():
            ring(OWN_Z - 1, X_STEPS[-1:])

        @pl.when(is_owner)
        def _():
            dst[p] = keep()

    def drain(sem, ref, count):
        window = ref.at[pl.ds(0, count)]
        pltpu.make_async_copy(window, window, sem).wait()

    def drain_tiles(sem, ref, count=TILES):
        @pl.when(is_owner)
        def _():
            drain(sem, ref, count - 1)

        @pl.when(jnp.logical_not(is_owner))
        def _():
            drain(sem, ref, count)

    cum_two[...] = jnp.zeros_like(cum_two)
    swap_cum.wait_recv()
    for i in range(2):
        own, other = cum_pad[pl.ds(mine + i, 1), :], cum_recv[pl.ds(mine + i, 1), :]
        cum_two[i : i + 1, :] = jnp.where(first, own, other)
        cum_two[2 + i : 3 + i, :] = jnp.where(first, other, own)
    logs = jnp.broadcast_to(cum_two[0:8, TOK - 1 : TOK], (8, DH))
    decays = jnp.exp(logs)
    first_decay = [decays[i : i + 1, :] for i in range(2)]
    second_decay = [decays[2 + i : 3 + i, :] for i in range(2)]
    for i in range(2):
        dec_src[i] = jnp.exp(logs[i : i + 1, :] + logs[2 + i : 3 + i, :])
    to_owners(lambda tile: dec_src.at[tile >> 4], dec_all, 0, lambda: dec_src[my_tile >> 4])

    swap_summ.wait_recv()
    for i in range(2):
        own, other = summ[mine + i], summ_recv[i]
        early = jnp.where(first, own, other)
        late = jnp.where(first, other, own)
        s_first[i] = early
        t_src[16 * i : 16 * i + 16] = (second_decay[i] * early + late).reshape(16, 8, DH)
    to_owners(lambda tile: t_src.at[tile], t_all, 1, lambda: t_src[my_tile])

    arrived(3, q)
    arrived(4, og)
    for n, rows in enumerate((q, k, v, og)):
        for i in range(2):
            in_src[n, i] = rows[theirs + i].astype(F32)
    swap_in = swap(2, in_src, in_recv)
    for rows, both in ((q, q2), (k, k2), (v, v2), (og, og2)):
        for i in range(2):
            both[mine + i] = rows[mine + i]
    cum_two_col[...] = cum_two[...].T
    arrived(5, gain)
    swap_in.wait_recv()
    for n, both in enumerate((q2, k2, v2, og2)):
        for i in range(2):
            both[theirs + i] = in_recv[n, i].astype(BF16)

    row_id = lax.broadcasted_iota(jnp.int32, (TOK, TOK), 0)
    col_id = lax.broadcasted_iota(jnp.int32, (TOK, TOK), 1)
    for j in range(4):
        col = cum_two_col[:, j : j + 1]
        spread = col - cum_two[j : j + 1, :]
        decay = jnp.where(row_id >= col_id, jnp.exp(jnp.minimum(spread, 0.0)), 0.0)
        dmat[j] = decay
        weights = (dot(q2[j], k2[j], NT) * decay).astype(BF16)
        wts[j] = weights
        attended[j] = dot(weights, v2[j], NN)
        growth[j] = jnp.broadcast_to(jnp.exp(col), (TOK, DH))
        qdec[j] = (q2[j].astype(F32) * growth[j]).astype(BF16)

    arrived(6, tile_in)
    arrived(7, tile_out)

    @pl.when(is_owner)
    def _():
        drain(a_recv.at[0], dec_all, CHIPS - 1)
        drain(a_recv.at[1], t_all, CHIPS - 1)

        def body(chip, state):
            p_src[chip] = state
            return dec_all[chip] * state + t_all[chip]

        lax.fori_loop(0, CHIPS, body, tile_in[...], unroll=4)
        to_chips(lambda chip: push(p_src.at[chip], p_ret.at[my_tile], 2, chip * 2 + c, y))
        p_ret[my_tile] = p_src[p]

    for j in range(4):
        gained[j] = gain[mine + j % 2] * og2[j].astype(F32)
    rows_pad[...] = jnp.zeros_like(rows_pad)

    drain_tiles(a_recv.at[2], p_ret)
    for i in range(2):
        chip_state = p_ret[16 * i : 16 * i + 16].reshape(DH, DH)
        states_bf[i] = chip_state.astype(BF16)
        states_bf[2 + i] = (first_decay[i] * chip_state + s_first[i]).astype(BF16)
    for block in range(2):
        square = jnp.zeros((TOK, DH), F32)
        inner = jnp.zeros((TOK, DH), F32)
        for j in (2 * block, 2 * block + 1):
            out = attended[j] + growth[j] * dot(q2[j], states_bf[j], NN)
            attended[j] = out
            square = square + out * out
            inner = inner + gained[j] * out
        sum_send[2 * block : 2 * block + 1, :] = jnp.sum(square.T, axis=0, keepdims=True)
        sum_send[2 * block + 1 : 2 * block + 2, :] = jnp.sum(inner.T, axis=0, keepdims=True)

    place = 2 * y + c
    for dy in Y_STEPS:
        for core in range(2):
            push(sum_send, sum_recv.at[place], 3, 2 * p + core, (y + dy) & (NY - 1))
    push(sum_send, sum_recv.at[place], 3, *partner)
    sum_recv[place] = sum_send[...]
    drain(a_recv.at[3], sum_recv, 2 * NY - 1)
    total = sum_recv[0]
    for i in range(1, 2 * NY):
        total = total + sum_recv[i]
    features = HL * DH * NY
    for block in range(2):
        inv_rms = lax.rsqrt(total[2 * block : 2 * block + 1, :] / features + EPSILON)
        coefficient = total[2 * block + 1 : 2 * block + 2, :] * (inv_rms * inv_rms * inv_rms) / features
        rows_pad[2 * block : 2 * block + 1, :] = inv_rms
        rows_pad[2 * block + 1 : 2 * block + 2, :] = coefficient
    cols_pad[...] = rows_pad[...].T

    for j in range(4):
        b = j // 2
        inv_col, coef_col = cols_pad[:, 2 * b : 2 * b + 1], cols_pad[:, 2 * b + 1 : 2 * b + 2]
        grad = (gained[j] * inv_col - attended[j] * coef_col).astype(BF16)
        agrad[j] = grad
        gsum[j] = dot(qdec[j], grad, TN)

    for i in range(2):
        u_src[16 * i : 16 * i + 16] = (first_decay[i] * gsum[2 + i] + gsum[i]).reshape(16, 8, DH)
    to_owners(lambda tile: u_src.at[tile], u_all, 4, lambda: u_src[my_tile])

    for j in range(4):
        score = (dot(agrad[j], v2[j], NT) * dmat[j]).astype(BF16)
        qpart[j] = dot(score, k2[j], NN) + growth[j] * dot(agrad[j], states_bf[j], NT)
        kpart[j] = dot(score, q2[j], TN)
        vpart[j] = dot(wts[j], agrad[j], TN)
    swap_parts = [
        swap(3 + n, part.at[pl.ds(theirs, 2)], dst)
        for n, (part, dst) in enumerate(((qpart, qpart_recv), (kpart, kpart_recv), (vpart, vpart_recv)))
    ]
    for i in range(2):
        qg[mine + i] = qpart[mine + i].astype(BF16)

    @pl.when(is_owner)
    def _():
        drain(a_recv.at[4], u_all, CHIPS - 1)

        def body(step, grad):
            chip = CHIPS - 1 - step
            h_src[chip] = grad
            return dec_all[chip] * grad + u_all[chip]

        g_src[...] = lax.fori_loop(0, CHIPS, body, tile_out[...], unroll=4)
        for dz in (6, 5, 7, 4, 8, 3, 9, 2, 10, 1, 11):
            zt = z + dz
            zt = jnp.where(zt >= NZ, zt - NZ, zt)
            push(g_src, g_all.at[c, my_tile], 6, (x * NZ + zt) * 2 + c, y)
        to_chips(lambda chip: push(h_src.at[chip], h_ret.at[my_tile], 5, chip * 2 + c, y))
        h_ret[my_tile] = h_src[p]
        g_all[c, my_tile] = g_src[...]

    for copy in swap_parts:
        copy.wait_recv()
    for i in range(2):
        qg[theirs + i] = qpart_recv[i].astype(BF16)

    drain_tiles(a_recv.at[6], g_all.at[c], OWN_Z)
    line = g_all.at[c, pl.ds(x * OWN_Z, OWN_Z)]
    for dx in X_STEPS[:-1]:
        push(line, line, 7, (xs[dx] * NZ + z) * 2 + c, y)

    drain_tiles(a_recv.at[5], h_ret)
    for i in range(2):
        after_second = h_ret[16 * i : 16 * i + 16].reshape(DH, DH)
        after_first = second_decay[i] * after_second + gsum[2 + i]
        h_fwd[i] = jnp.where(first, after_second, after_first)
        grads_bf[mine + i] = jnp.where(first, after_first, after_second).astype(BF16)
    swap_back = swap(6, h_fwd, h_other)

    def finish(h, key_part, value_part):
        kg[h] = (key_part + shrink[h] * dot(v[h], grads_bf[h], NT)).astype(BF16)
        vg[h] = (value_part + shrink[h] * dot(k[h], grads_bf[h], NN)).astype(BF16)

    for i in range(2):
        finish(mine + i, kpart[mine + i], vpart[mine + i])
    swap_back.wait_recv()
    for i in range(2):
        grads_bf[theirs + i] = h_other[i].astype(BF16)
    for i in range(2):
        finish(theirs + i, kpart_recv[i], vpart_recv[i])

    drain(a_recv.at[7], g_all.at[c], TILES - OWN_Z)
    swap_slab = swap(7, g_all.at[c], g_all.at[c])
    swap_slab.wait_recv()
    sg[...] = g_all[...]

    for copy in (swap_cum, swap_summ, swap_in, *swap_parts, swap_back, swap_slab):
        copy.wait_send()
    for slot, ref in ((0, dec_all), (1, t_src), (4, u_src)):
        drain_tiles(a_send.at[slot], ref)
    drain(a_send.at[3], sum_recv, 2 * NY - 1)

    @pl.when(is_owner)
    def _():
        for slot in (2, 5):
            drain(a_send.at[slot], p_src, CHIPS - 1)
        drain(a_send.at[6], p_src, NZ - 1)

    drain(a_send.at[7], p_src, TILES - OWN_Z)


def store_kernel(qg, kg, vg, sg, qg_out, kg_out, vg_out, sg_out, sem):
    copies = [pltpu.make_async_copy(sg, sg_out, sem.at[3 * HL])]
    for index, (src, dst) in enumerate(((qg, qg_out), (kg, kg_out), (vg, vg_out))):
        for h in range(HL):
            copies.append(pltpu.make_async_copy(src.at[h], dst.at[:, pl.ds(h * DH, DH)], sem.at[index * HL + h]))
    for copy in copies:
        copy.start()
    for copy in copies:
        copy.wait()


def on_device(query_rows, key_rows, value_rows, log_decay, out_grad, norm_gain, state_in, state_out_grad):
    hbm = pl.BlockSpec(memory_space=pltpu.HBM)
    vmem = pl.BlockSpec(memory_space=pltpu.VMEM)

    def vm(*shape, dtype=F32):
        return pltpu.VMEM(shape, dtype)

    tiles = vm(TILES, 8, DH)
    landing = vm(CHIPS, 8, DH)
    pair = vm(2, DH, DH)
    heads = vm(HL, TOK, DH)
    block_pair = vm(2, TOK, DH)
    heads_bf = vm(HL, TOK, DH, dtype=BF16)
    state = vm(HL, DH, DH)
    state_bf = vm(HL, DH, DH, dtype=BF16)
    dma = pltpu.SemaphoreType.DMA
    rows = jax.ShapeDtypeStruct(query_rows.shape, BF16)
    slab = jax.ShapeDtypeStruct((2, TILES, 8, DH), F32)
    by_head = vm(HL, TOK, DH, dtype=BF16)
    arrays = (
        query_rows, key_rows, value_rows, log_decay, out_grad, norm_gain.reshape(HL, 1, DH),
        state_in.reshape(2 * TILES, 8, DH), state_out_grad.reshape(2 * TILES, 8, DH),
    )
    grads = pl.pallas_call(
        kernel,
        out_shape=(by_head, by_head, by_head, vm(2, TILES, 8, DH)),
        in_specs=[hbm] * 8,
        out_specs=(vmem,) * 4,
        scratch_shapes=[
            heads_bf, heads_bf, heads_bf, heads_bf, vm(HL, 1, DH), vm(HL, TOK), vm(8, DH), vm(8, DH),
            vm(DH, TOK), vm(TOK, DH), vm(8, TOK), vm(DH, TOK), vm(TOK, DH), vm(2, 1, DH), vm(CHIPS, 1, DH),
            vm(4, TOK), vm(2 * NY, 4, TOK), vm(DH, TOK), vm(TOK, DH),
            state, pair, pair, tiles, landing, landing, tiles,
            state, tiles, landing, landing, tiles, pair, pair, vm(8, DH), vm(2, TILES, 8, DH),
            vm(4, 2, TOK, DH), vm(4, 2, TOK, DH), heads_bf, heads_bf, heads_bf, heads_bf,
            state_bf, state_bf, vm(HL, TOK, TOK), vm(HL, TOK, TOK, dtype=BF16), heads, heads, heads, heads, heads_bf, heads_bf,
            heads, heads, heads, block_pair, block_pair, block_pair,
            dma((8,)), dma((8,)), dma((8,)), dma((8,)), dma((8,)),
        ],
        compiler_params=pltpu.CompilerParams(
            collective_id=0, has_side_effects=True, vmem_limit_bytes=32 * 1024 * 1024
        ),
    )(*(pltpu.with_memory_space_constraint(array, pltpu.HBM) for array in arrays))
    qg, kg, vg, sg = pl.pallas_call(
        store_kernel,
        out_shape=(rows, rows, rows, slab),
        in_specs=[vmem] * 4,
        out_specs=(hbm,) * 4,
        scratch_shapes=[dma((3 * HL + 1,))],
        compiler_params=pltpu.CompilerParams(vmem_limit_bytes=4 * 1024 * 1024),
    )(*(pltpu.with_memory_space_constraint(grad, pltpu.VMEM) for grad in grads))
    return qg, kg, vg, sg.reshape(HL, DH, DH)


def solution(mesh):
    wide = P("seq", "head")
    state = P("head", None, None)
    return jax.shard_map(
        on_device,
        mesh=mesh,
        in_specs=(wide, wide, wide, P("head", "seq"), wide, P("head"), state, state),
        out_specs=(wide, wide, wide, state),
        check_vma=False,
    )
```

```python
import jax
import jax.numpy as jnp
from jax import lax
from jax.experimental import pallas as pl
from jax.experimental.pallas import tpu as pltpu
from jax.sharding import PartitionSpec as P

EPSILON = 1e-06
MESH = pl.DeviceIdType.MESH
F32 = jnp.float32
BF16 = jnp.bfloat16

NX, NZ, NY = 4, 12, 8
CHIPS = NX * NZ
HL, TOK, DH = 4, 256, 128
TILES = 32
OWN_Z = 8
X_STEPS = (2, 1, 3, 0)
Y_STEPS = (4, 3, 5, 2, 6, 1, 7)


def far_first(step, count):
    return count // 2 + ((step + 1) >> 1) * (1 - 2 * (step & 1))


def dot(a, b, dims):
    return lax.dot_general(a, b, (dims, ((), ())), preferred_element_type=F32)


NN = ((1,), (0,))
NT = ((1,), (1,))
TN = ((0,), (0,))


def at_least(value, bounds):
    return sum((value >= bound).astype(jnp.int32) for bound in bounds)


def kernel(
    q_hbm, k_hbm, v_hbm, ld_hbm, og_hbm, gain_hbm, sin_hbm, sout_hbm,
    qg, kg, vg, sg,
    q, k, v, og, gain, ld, tile_in, tile_out,
    cum_pad, cum_col, cum_recv, cum_two, cum_two_col, dec_src, dec_all,
    sum_send, sum_recv, rows_pad, cols_pad,
    summ, summ_recv, s_first, t_src, t_all, p_src, p_ret,
    gsum, u_src, u_all, h_src, h_ret, h_fwd, h_other, g_src, g_all,
    in_src, in_recv, q2, k2, v2, og2,
    states_bf, grads_bf, dmat, wts, growth, shrink, attended, gained, qdec_t, agrad,
    qpart, kpart, vpart, qpart_recv, kpart_recv, vpart_recv,
    in_sem, x_send, x_recv, a_send, a_recv,
):
    s = lax.axis_index("seq")
    y = lax.axis_index("head")
    c = s & 1
    p = s >> 1
    x = at_least(p, (NZ, 2 * NZ, 3 * NZ))
    z = p - NZ * x
    third = at_least(z, (3, 6, 9))
    z_rest = z - 3 * third
    is_owner = z_rest != 2
    zi = 2 * third + jnp.minimum(z_rest, 1)
    my_tile = x * OWN_Z + zi
    partner = (s + 1 - 2 * c, y)
    mine, theirs = 2 * c, 2 - 2 * c
    first = c == 0
    xs = {dx: (x + dx) & (NX - 1) for dx in X_STEPS}

    def load(slot, *pairs):
        for src, dst in pairs:
            pltpu.make_async_copy(src, dst, in_sem.at[slot]).start()

    def arrived(slot, dst):
        pltpu.make_async_copy(dst, dst, in_sem.at[slot]).wait()

    def load_heads(slot, src, dst):
        load(slot, *((src.at[:, pl.ds(h * DH, DH)], dst.at[h]) for h in range(HL)))

    load(0, (ld_hbm, ld))
    load_heads(1, k_hbm, k)
    load_heads(2, v_hbm, v)
    load_heads(3, q_hbm, q)
    load_heads(4, og_hbm, og)
    load(5, (gain_hbm, gain))
    load(6, (sin_hbm.at[c * TILES + my_tile], tile_in))
    load(7, (sout_hbm.at[c * TILES + my_tile], tile_out))

    def to_chips(send):
        def ring(step, steps):
            zt = z + far_first(step, NZ)
            zt = jnp.where(zt >= NZ, zt - NZ, zt)
            for dx in steps:
                send(xs[dx] * NZ + zt)

        def body(step, carry):
            ring(step, X_STEPS)
            return carry

        lax.fori_loop(0, NZ - 1, body, 0)
        ring(NZ - 1, X_STEPS[:-1])

    barrier = pltpu.get_barrier_semaphore()

    def greet(s_there, y_there):
        pl.semaphore_signal(barrier, inc=1, device_id=(s_there, y_there), device_id_type=MESH)

    to_chips(lambda chip: greet(chip * 2 + c, y))
    for dy in Y_STEPS:
        for core in range(2):
            greet(2 * p + core, (y + dy) & (NY - 1))
    greet(*partner)

    cum_pad[...] = jnp.zeros_like(cum_pad)
    arrived(0, ld)
    cum_pad[0:HL, :] = ld[...]
    cum = cum_pad[0:8, :]
    lane = lax.broadcasted_iota(jnp.int32, (8, TOK), 1)
    for shift in (1, 2, 4, 8, 16, 32, 64, 128):
        cum = cum + jnp.where(lane >= shift, pltpu.roll(cum, shift, 1), 0.0)
    cum_pad[0:8, :] = cum
    cum_col[...] = cum_pad[...].T

    arrived(1, k)
    arrived(2, v)
    for h in range(HL):
        fade = jnp.exp(cum_col[TOK - 1 : TOK, h : h + 1] - cum_col[:, h : h + 1])
        shrink[h] = jnp.broadcast_to(fade, (TOK, DH))
        key_decayed = (k[h].astype(F32) * shrink[h]).astype(BF16)
        summ[h] = dot(key_decayed, v[h], TN)

    pl.semaphore_wait(barrier, CHIPS - 1 + 2 * NY - 1)

    def swap(slot, src, dst):
        copy = pltpu.make_async_remote_copy(
            src_ref=src, dst_ref=dst, send_sem=x_send.at[slot], recv_sem=x_recv.at[slot],
            device_id=partner, device_id_type=MESH,
        )
        copy.start()
        return copy

    swap_cum = swap(0, cum_pad.at[pl.ds(0, 8)], cum_recv)
    swap_summ = swap(1, summ.at[pl.ds(theirs, 2)], summ_recv)

    def push(src, dst, slot, s_there, y_there):
        pltpu.make_async_remote_copy(
            src_ref=src, dst_ref=dst, send_sem=a_send.at[slot], recv_sem=a_recv.at[slot],
            device_id=(s_there, y_there), device_id_type=MESH,
        ).start()

    def to_owners(src_of, dst, slot, keep):
        def ring(step, steps):
            zt = (zi + far_first(step, OWN_Z)) & (OWN_Z - 1)
            z_there = (zt >> 1) * 3 + (zt & 1)
            for dx in steps:
                push(src_of(xs[dx] * OWN_Z + zt), dst.at[p], slot, (xs[dx] * NZ + z_there) * 2 + c, y)

        def body(step, carry):
            ring(step, X_STEPS)
            return carry

        lax.fori_loop(0, OWN_Z - 1, body, 0)
        ring(OWN_Z - 1, X_STEPS[:-1])

        @pl.when(jnp.logical_not(is_owner))
        def _():
            ring(OWN_Z - 1, X_STEPS[-1:])

        @pl.when(is_owner)
        def _():
            dst[p] = keep()

    def drain(sem, ref, count):
        window = ref.at[pl.ds(0, count)]
        pltpu.make_async_copy(window, window, sem).wait()

    def drain_tiles(sem, ref, count=TILES):
        @pl.when(is_owner)
        def _():
            drain(sem, ref, count - 1)

        @pl.when(jnp.logical_not(is_owner))
        def _():
            drain(sem, ref, count)

    cum_two[...] = jnp.zeros_like(cum_two)
    swap_cum.wait_recv()
    for i in range(2):
        own, other = cum_pad[pl.ds(mine + i, 1), :], cum_recv[pl.ds(mine + i, 1), :]
        cum_two[i : i + 1, :] = jnp.where(first, own, other)
        cum_two[2 + i : 3 + i, :] = jnp.where(first, other, own)
    logs = jnp.broadcast_to(cum_two[0:8, TOK - 1 : TOK], (8, DH))
    decays = jnp.exp(logs)
    first_decay = [decays[i : i + 1, :] for i in range(2)]
    second_decay = [decays[2 + i : 3 + i, :] for i in range(2)]
    for i in range(2):
        dec_src[i] = jnp.exp(logs[i : i + 1, :] + logs[2 + i : 3 + i, :])
    to_owners(lambda tile: dec_src.at[tile >> 4], dec_all, 0, lambda: dec_src[my_tile >> 4])

    swap_summ.wait_recv()
    for i in range(2):
        own, other = summ[mine + i], summ_recv[i]
        early = jnp.where(first, own, other)
        late = jnp.where(first, other, own)
        s_first[i] = early
        t_src[16 * i : 16 * i + 16] = (second_decay[i] * early + late).reshape(16, 8, DH)
    to_owners(lambda tile: t_src.at[tile], t_all, 1, lambda: t_src[my_tile])

    arrived(3, q)
    arrived(4, og)
    for n, rows in enumerate((q, k, v, og)):
        for i in range(2):
            in_src[n, i] = rows[theirs + i].astype(F32)
    swap_in = swap(2, in_src, in_recv)
    for rows, both in ((q, q2), (k, k2), (v, v2), (og, og2)):
        for i in range(2):
            both[mine + i] = rows[mine + i]
    cum_two_col[...] = cum_two[...].T
    arrived(5, gain)
    swap_in.wait_recv()
    for n, both in enumerate((q2, k2, v2, og2)):
        for i in range(2):
            both[theirs + i] = in_recv[n, i].astype(BF16)

    row_id = lax.broadcasted_iota(jnp.int32, (TOK, TOK), 0)
    col_id = lax.broadcasted_iota(jnp.int32, (TOK, TOK), 1)
    for j in range(4):
        col = cum_two_col[:, j : j + 1]
        spread = col - cum_two[j : j + 1, :]
        decay = jnp.where(row_id >= col_id, jnp.exp(jnp.minimum(spread, 0.0)), 0.0)
        dmat[j] = decay
        weights = (dot(q2[j], k2[j], NT) * decay).astype(BF16)
        wts[j] = weights
        attended[j] = dot(weights, v2[j], NN)
        growth[j] = jnp.broadcast_to(jnp.exp(col), (TOK, DH))
        qdec_t[j] = (q2[j].astype(F32) * growth[j]).T.astype(BF16)

    arrived(6, tile_in)
    arrived(7, tile_out)

    @pl.when(is_owner)
    def _():
        drain(a_recv.at[0], dec_all, CHIPS - 1)
        drain(a_recv.at[1], t_all, CHIPS - 1)

        def body(chip, state):
            p_src[chip] = state
            return dec_all[chip] * state + t_all[chip]

        lax.fori_loop(0, CHIPS, body, tile_in[...], unroll=4)
        to_chips(lambda chip: push(p_src.at[chip], p_ret.at[my_tile], 2, chip * 2 + c, y))
        p_ret[my_tile] = p_src[p]

    for j in range(4):
        gained[j] = gain[mine + j % 2] * og2[j].astype(F32)
    rows_pad[...] = jnp.zeros_like(rows_pad)

    drain_tiles(a_recv.at[2], p_ret)
    for i in range(2):
        chip_state = p_ret[16 * i : 16 * i + 16].reshape(DH, DH)
        states_bf[i] = chip_state.astype(BF16)
        states_bf[2 + i] = (first_decay[i] * chip_state + s_first[i]).astype(BF16)
    for block in range(2):
        square = jnp.zeros((TOK, DH), F32)
        inner = jnp.zeros((TOK, DH), F32)
        for j in (2 * block, 2 * block + 1):
            out = attended[j] + growth[j] * dot(q2[j], states_bf[j], NN)
            attended[j] = out
            square = square + out * out
            inner = inner + gained[j] * out
        sum_send[2 * block : 2 * block + 1, :] = jnp.sum(square.T, axis=0, keepdims=True)
        sum_send[2 * block + 1 : 2 * block + 2, :] = jnp.sum(inner.T, axis=0, keepdims=True)

    place = 2 * y + c
    for dy in Y_STEPS:
        for core in range(2):
            push(sum_send, sum_recv.at[place], 3, 2 * p + core, (y + dy) & (NY - 1))
    push(sum_send, sum_recv.at[place], 3, *partner)
    sum_recv[place] = sum_send[...]
    drain(a_recv.at[3], sum_recv, 2 * NY - 1)
    total = sum_recv[0]
    for i in range(1, 2 * NY):
        total = total + sum_recv[i]
    features = HL * DH * NY
    for block in range(2):
        inv_rms = lax.rsqrt(total[2 * block : 2 * block + 1, :] / features + EPSILON)
        coefficient = total[2 * block + 1 : 2 * block + 2, :] * (inv_rms * inv_rms * inv_rms) / features
        rows_pad[2 * block : 2 * block + 1, :] = inv_rms
        rows_pad[2 * block + 1 : 2 * block + 2, :] = coefficient
    cols_pad[...] = rows_pad[...].T

    for block in range(2):
        inv_wide = jnp.broadcast_to(cols_pad[:, 2 * block : 2 * block + 1], (TOK, DH))
        coef_wide = jnp.broadcast_to(cols_pad[:, 2 * block + 1 : 2 * block + 2], (TOK, DH))
        for j in (2 * block, 2 * block + 1):
            grad = (gained[j] * inv_wide - attended[j] * coef_wide).astype(BF16)
            agrad[j] = grad
            gsum[j] = dot(qdec_t[j], grad, NN)

    for i in range(2):
        u_src[16 * i : 16 * i + 16] = (first_decay[i] * gsum[2 + i] + gsum[i]).reshape(16, 8, DH)
    to_owners(lambda tile: u_src.at[tile], u_all, 4, lambda: u_src[my_tile])

    for j in range(4):
        score = (dot(agrad[j], v2[j], NT) * dmat[j]).astype(BF16)
        qpart[j] = dot(score, k2[j], NN) + growth[j] * dot(agrad[j], states_bf[j], NT)
        kpart[j] = dot(score, q2[j], TN)
        vpart[j] = dot(wts[j], agrad[j], TN)
    swap_parts = [
        swap(3 + n, part.at[pl.ds(theirs, 2)], dst)
        for n, (part, dst) in enumerate(((qpart, qpart_recv), (kpart, kpart_recv), (vpart, vpart_recv)))
    ]
    for i in range(2):
        qg[mine + i] = qpart[mine + i].astype(BF16)

    @pl.when(is_owner)
    def _():
        drain(a_recv.at[4], u_all, CHIPS - 1)

        def body(step, grad):
            chip = CHIPS - 1 - step
            h_src[chip] = grad
            return dec_all[chip] * grad + u_all[chip]

        g_src[...] = lax.fori_loop(0, CHIPS, body, tile_out[...], unroll=4)
        for dz in (6, 5, 7, 4, 8, 3, 9, 2, 10, 1, 11):
            zt = z + dz
            zt = jnp.where(zt >= NZ, zt - NZ, zt)
            push(g_src, g_all.at[c, my_tile], 6, (x * NZ + zt) * 2 + c, y)
        to_chips(lambda chip: push(h_src.at[chip], h_ret.at[my_tile], 5, chip * 2 + c, y))
        h_ret[my_tile] = h_src[p]
        g_all[c, my_tile] = g_src[...]

    for copy in swap_parts:
        copy.wait_recv()
    for i in range(2):
        qg[theirs + i] = qpart_recv[i].astype(BF16)

    drain_tiles(a_recv.at[6], g_all.at[c], OWN_Z)
    line = g_all.at[c, pl.ds(x * OWN_Z, OWN_Z)]
    for dx in X_STEPS[:-1]:
        push(line, line, 6 + dx, (xs[dx] * NZ + z) * 2 + c, y)
    swap_lines = [swap(7, line, line)]

    drain_tiles(a_recv.at[5], h_ret)
    for i in range(2):
        after_second = h_ret[16 * i : 16 * i + 16].reshape(DH, DH)
        after_first = second_decay[i] * after_second + gsum[2 + i]
        h_fwd[i] = jnp.where(first, after_second, after_first)
        grads_bf[mine + i] = jnp.where(first, after_first, after_second).astype(BF16)
    swap_back = swap(6, h_fwd, h_other)

    def finish(h, key_part, value_part):
        kg[h] = (key_part + shrink[h] * dot(v[h], grads_bf[h], NT)).astype(BF16)
        vg[h] = (value_part + shrink[h] * dot(k[h], grads_bf[h], NN)).astype(BF16)

    for i in range(2):
        finish(mine + i, kpart[mine + i], vpart[mine + i])
    swap_back.wait_recv()
    for i in range(2):
        grads_bf[theirs + i] = h_other[i].astype(BF16)
    for i in range(2):
        finish(theirs + i, kpart_recv[i], vpart_recv[i])

    for dx in (1, 3, 2):
        drain(a_recv.at[6 + dx], g_all.at[c], OWN_Z)
        line = g_all.at[c, pl.ds(((x - dx) & (NX - 1)) * OWN_Z, OWN_Z)]
        swap_lines.append(swap(7 + dx, line, line))
    for copy in swap_lines:
        copy.wait_recv()
    sg[...] = g_all[...]

    for copy in (swap_cum, swap_summ, swap_in, *swap_parts, swap_back, *swap_lines):
        copy.wait_send()
    for slot, ref in ((0, dec_all), (1, t_src), (4, u_src)):
        drain_tiles(a_send.at[slot], ref)
    drain(a_send.at[3], sum_recv, 2 * NY - 1)

    @pl.when(is_owner)
    def _():
        for slot in (2, 5):
            drain(a_send.at[slot], p_src, CHIPS - 1)
        drain(a_send.at[6], p_src, NZ - 1)

    for dx in (1, 3, 2):
        drain(a_send.at[6 + dx], p_src, OWN_Z)


def store_kernel(qg, kg, vg, sg, qg_out, kg_out, vg_out, sg_out, sem):
    copies = [pltpu.make_async_copy(sg, sg_out, sem.at[3 * HL])]
    for index, (src, dst) in enumerate(((qg, qg_out), (kg, kg_out), (vg, vg_out))):
        for h in range(HL):
            copies.append(pltpu.make_async_copy(src.at[h], dst.at[:, pl.ds(h * DH, DH)], sem.at[index * HL + h]))
    for copy in copies:
        copy.start()
    for copy in copies:
        copy.wait()


def on_device(query_rows, key_rows, value_rows, log_decay, out_grad, norm_gain, state_in, state_out_grad):
    hbm = pl.BlockSpec(memory_space=pltpu.HBM)
    vmem = pl.BlockSpec(memory_space=pltpu.VMEM)

    def vm(*shape, dtype=F32):
        return pltpu.VMEM(shape, dtype)

    tiles = vm(TILES, 8, DH)
    landing = vm(CHIPS, 8, DH)
    pair = vm(2, DH, DH)
    heads = vm(HL, TOK, DH)
    block_pair = vm(2, TOK, DH)
    heads_bf = vm(HL, TOK, DH, dtype=BF16)
    state = vm(HL, DH, DH)
    state_bf = vm(HL, DH, DH, dtype=BF16)
    dma = pltpu.SemaphoreType.DMA
    rows = jax.ShapeDtypeStruct(query_rows.shape, BF16)
    slab = jax.ShapeDtypeStruct((2, TILES, 8, DH), F32)
    by_head = vm(HL, TOK, DH, dtype=BF16)
    arrays = (
        query_rows, key_rows, value_rows, log_decay, out_grad, norm_gain.reshape(HL, 1, DH),
        state_in.reshape(2 * TILES, 8, DH), state_out_grad.reshape(2 * TILES, 8, DH),
    )
    grads = pl.pallas_call(
        kernel,
        out_shape=(by_head, by_head, by_head, vm(2, TILES, 8, DH)),
        in_specs=[hbm] * 8,
        out_specs=(vmem,) * 4,
        scratch_shapes=[
            heads_bf, heads_bf, heads_bf, heads_bf, vm(HL, 1, DH), vm(HL, TOK), vm(8, DH), vm(8, DH),
            vm(DH, TOK), vm(TOK, DH), vm(8, TOK), vm(DH, TOK), vm(TOK, DH), vm(2, 1, DH), vm(CHIPS, 1, DH),
            vm(4, TOK), vm(2 * NY, 4, TOK), vm(DH, TOK), vm(TOK, DH),
            state, pair, pair, tiles, landing, landing, tiles,
            state, tiles, landing, landing, tiles, pair, pair, vm(8, DH), vm(2, TILES, 8, DH),
            vm(4, 2, TOK, DH), vm(4, 2, TOK, DH), heads_bf, heads_bf, heads_bf, heads_bf,
            state_bf, state_bf, vm(HL, TOK, TOK), vm(HL, TOK, TOK, dtype=BF16), heads, heads, heads, heads, vm(HL, DH, TOK, dtype=BF16), heads_bf,
            heads, heads, heads, block_pair, block_pair, block_pair,
            dma((8,)), dma((11,)), dma((11,)), dma((10,)), dma((10,)),
        ],
        compiler_params=pltpu.CompilerParams(
            collective_id=0, has_side_effects=True, vmem_limit_bytes=32 * 1024 * 1024
        ),
    )(*(pltpu.with_memory_space_constraint(array, pltpu.HBM) for array in arrays))
    qg, kg, vg, sg = pl.pallas_call(
        store_kernel,
        out_shape=(rows, rows, rows, slab),
        in_specs=[vmem] * 4,
        out_specs=(hbm,) * 4,
        scratch_shapes=[dma((3 * HL + 1,))],
        compiler_params=pltpu.CompilerParams(vmem_limit_bytes=4 * 1024 * 1024),
    )(*(pltpu.with_memory_space_constraint(grad, pltpu.VMEM) for grad in grads))
    return qg, kg, vg, sg.reshape(HL, DH, DH)


def solution(mesh):
    wide = P("seq", "head")
    state = P("head", None, None)
    return jax.shard_map(
        on_device,
        mesh=mesh,
        in_specs=(wide, wide, wide, P("head", "seq"), wide, P("head"), state, state),
        out_specs=(wide, wide, wide, state),
        check_vma=False,
    )
```

```python
import jax
import jax.numpy as jnp
from jax import lax
from jax.experimental import pallas as pl
from jax.experimental.pallas import tpu as pltpu
from jax.sharding import PartitionSpec as P

EPSILON = 1e-06
MESH = pl.DeviceIdType.MESH
F32 = jnp.float32
BF16 = jnp.bfloat16

NX, NZ, NY = 4, 12, 8
CHIPS = NX * NZ
HL, TOK, DH = 4, 256, 128
TILES = 32
OWN_Z = 8
X_STEPS = (2, 1, 3, 0)
Y_STEPS = (4, 3, 5, 2, 6, 1, 7)


def far_first(step, count):
    return count // 2 + ((step + 1) >> 1) * (1 - 2 * (step & 1))


def dot(a, b, dims):
    return lax.dot_general(a, b, (dims, ((), ())), preferred_element_type=F32)


NN = ((1,), (0,))
NT = ((1,), (1,))
TN = ((0,), (0,))


def at_least(value, bounds):
    return sum((value >= bound).astype(jnp.int32) for bound in bounds)


def kernel(
    q_hbm, k_hbm, v_hbm, ld_hbm, og_hbm, gain_hbm, sin_hbm, sout_hbm,
    qg, kg, vg, sg,
    q, k, v, og, gain, ld, tile_in, tile_out,
    cum_pad, cum_col, cum_recv, cum_two, cum_two_col, dec_src, dec_all,
    sum_send, sum_recv, rows_pad, cols_pad,
    summ, summ_recv, s_first, t_src, t_all, p_src, p_ret,
    gsum, u_src, u_all, h_src, h_ret, h_fwd, h_other, g_src, g_all,
    in_src, in_recv, q2, k2, v2, og2,
    states_bf, grads_bf, dmat, wts, growth, shrink, attended, gained, qdec_t, agrad,
    qpart, kpart, vpart, qpart_recv, kpart_recv, vpart_recv,
    in_sem, x_send, x_recv, a_send, a_recv,
):
    s = lax.axis_index("seq")
    y = lax.axis_index("head")
    c = s & 1
    p = s >> 1
    x = at_least(p, (NZ, 2 * NZ, 3 * NZ))
    z = p - NZ * x
    third = at_least(z, (3, 6, 9))
    z_rest = z - 3 * third
    is_owner = z_rest != 2
    zi = 2 * third + jnp.minimum(z_rest, 1)
    my_tile = x * OWN_Z + zi
    partner = (s + 1 - 2 * c, y)
    mine, theirs = 2 * c, 2 - 2 * c
    first = c == 0
    xs = {dx: (x + dx) & (NX - 1) for dx in X_STEPS}

    def load(slot, *pairs):
        for src, dst in pairs:
            pltpu.make_async_copy(src, dst, in_sem.at[slot]).start()

    def arrived(slot, dst):
        pltpu.make_async_copy(dst, dst, in_sem.at[slot]).wait()

    def load_heads(slot, src, dst):
        load(slot, *((src.at[:, pl.ds(h * DH, DH)], dst.at[h]) for h in range(HL)))

    load(0, (ld_hbm, ld))
    load_heads(1, k_hbm, k)
    load_heads(2, v_hbm, v)
    load_heads(3, q_hbm, q)
    load_heads(4, og_hbm, og)
    load(5, (gain_hbm, gain))
    load(6, (sin_hbm.at[c * TILES + my_tile], tile_in))
    load(7, (sout_hbm.at[c * TILES + my_tile], tile_out))

    def to_chips(send):
        def ring(step, steps):
            zt = z + far_first(step, NZ)
            zt = jnp.where(zt >= NZ, zt - NZ, zt)
            for dx in steps:
                send(xs[dx] * NZ + zt)

        def body(step, carry):
            ring(step, X_STEPS)
            return carry

        lax.fori_loop(0, NZ - 1, body, 0)
        ring(NZ - 1, X_STEPS[:-1])

    barrier = pltpu.get_barrier_semaphore()

    def greet(s_there, y_there):
        pl.semaphore_signal(barrier, inc=1, device_id=(s_there, y_there), device_id_type=MESH)

    to_chips(lambda chip: greet(chip * 2 + c, y))
    for dy in Y_STEPS:
        for core in range(2):
            greet(2 * p + core, (y + dy) & (NY - 1))
    greet(*partner)

    cum_pad[...] = jnp.zeros_like(cum_pad)
    arrived(0, ld)
    cum_pad[0:HL, :] = ld[...]
    cum = cum_pad[0:8, :]
    lane = lax.broadcasted_iota(jnp.int32, (8, TOK), 1)
    for shift in (1, 2, 4, 8, 16, 32, 64, 128):
        cum = cum + jnp.where(lane >= shift, pltpu.roll(cum, shift, 1), 0.0)
    cum_pad[0:8, :] = cum
    cum_col[...] = cum_pad[...].T

    arrived(1, k)
    arrived(2, v)
    for h in range(HL):
        fade = jnp.exp(cum_col[TOK - 1 : TOK, h : h + 1] - cum_col[:, h : h + 1])
        shrink[h] = jnp.broadcast_to(fade, (TOK, DH))
        key_decayed = (k[h].astype(F32) * shrink[h]).astype(BF16)
        summ[h] = dot(key_decayed, v[h], TN)

    pl.semaphore_wait(barrier, CHIPS - 1 + 2 * NY - 1)

    def swap(slot, src, dst):
        copy = pltpu.make_async_remote_copy(
            src_ref=src, dst_ref=dst, send_sem=x_send.at[slot], recv_sem=x_recv.at[slot],
            device_id=partner, device_id_type=MESH,
        )
        copy.start()
        return copy

    swap_cum = swap(0, cum_pad.at[pl.ds(0, 8)], cum_recv)
    swap_summ = swap(1, summ.at[pl.ds(theirs, 2)], summ_recv)

    def push(src, dst, slot, s_there, y_there):
        pltpu.make_async_remote_copy(
            src_ref=src, dst_ref=dst, send_sem=a_send.at[slot], recv_sem=a_recv.at[slot],
            device_id=(s_there, y_there), device_id_type=MESH,
        ).start()

    def to_owners(src_of, dst, slot, keep):
        def ring(step, steps):
            zt = (zi + far_first(step, OWN_Z)) & (OWN_Z - 1)
            z_there = (zt >> 1) * 3 + (zt & 1)
            for dx in steps:
                push(src_of(xs[dx] * OWN_Z + zt), dst.at[p], slot, (xs[dx] * NZ + z_there) * 2 + c, y)

        def body(step, carry):
            ring(step, X_STEPS)
            return carry

        lax.fori_loop(0, OWN_Z - 1, body, 0)
        ring(OWN_Z - 1, X_STEPS[:-1])

        @pl.when(jnp.logical_not(is_owner))
        def _():
            ring(OWN_Z - 1, X_STEPS[-1:])

        @pl.when(is_owner)
        def _():
            dst[p] = keep()

    def drain(sem, ref, count):
        window = ref.at[pl.ds(0, count)]
        pltpu.make_async_copy(window, window, sem).wait()

    def drain_tiles(sem, ref, count=TILES):
        @pl.when(is_owner)
        def _():
            drain(sem, ref, count - 1)

        @pl.when(jnp.logical_not(is_owner))
        def _():
            drain(sem, ref, count)

    cum_two[...] = jnp.zeros_like(cum_two)
    swap_cum.wait_recv()
    for i in range(2):
        own, other = cum_pad[pl.ds(mine + i, 1), :], cum_recv[pl.ds(mine + i, 1), :]
        cum_two[i : i + 1, :] = jnp.where(first, own, other)
        cum_two[2 + i : 3 + i, :] = jnp.where(first, other, own)
    logs = jnp.broadcast_to(cum_two[0:8, TOK - 1 : TOK], (8, DH))
    decays = jnp.exp(logs)
    first_decay = [decays[i : i + 1, :] for i in range(2)]
    second_decay = [decays[2 + i : 3 + i, :] for i in range(2)]
    for i in range(2):
        dec_src[i] = jnp.exp(logs[i : i + 1, :] + logs[2 + i : 3 + i, :])
    to_owners(lambda tile: dec_src.at[tile >> 4], dec_all, 0, lambda: dec_src[my_tile >> 4])

    swap_summ.wait_recv()
    for i in range(2):
        own, other = summ[mine + i], summ_recv[i]
        early = jnp.where(first, own, other)
        late = jnp.where(first, other, own)
        s_first[i] = early
        t_src[16 * i : 16 * i + 16] = (second_decay[i] * early + late).reshape(16, 8, DH)
    to_owners(lambda tile: t_src.at[tile], t_all, 1, lambda: t_src[my_tile])

    arrived(6, tile_in)
    arrived(7, tile_out)

    @pl.when(is_owner)
    def _():
        drain(a_recv.at[0], dec_all, CHIPS - 1)
        drain(a_recv.at[1], t_all, CHIPS - 1)

        def body(chip, state):
            p_src[chip] = state
            return dec_all[chip] * state + t_all[chip]

        lax.fori_loop(0, CHIPS, body, tile_in[...], unroll=4)
        to_chips(lambda chip: push(p_src.at[chip], p_ret.at[my_tile], 2, chip * 2 + c, y))
        p_ret[my_tile] = p_src[p]

    arrived(3, q)
    arrived(4, og)
    for n, rows in enumerate((q, k, v, og)):
        for i in range(2):
            in_src[n, i] = rows[theirs + i].astype(F32)
    swap_in = swap(2, in_src, in_recv)
    for rows, both in ((q, q2), (k, k2), (v, v2), (og, og2)):
        for i in range(2):
            both[mine + i] = rows[mine + i]
    cum_two_col[...] = cum_two[...].T
    arrived(5, gain)
    swap_in.wait_recv()
    for n, both in enumerate((q2, k2, v2, og2)):
        for i in range(2):
            both[theirs + i] = in_recv[n, i].astype(BF16)

    row_id = lax.broadcasted_iota(jnp.int32, (TOK, TOK), 0)
    col_id = lax.broadcasted_iota(jnp.int32, (TOK, TOK), 1)
    for j in range(4):
        col = cum_two_col[:, j : j + 1]
        spread = col - cum_two[j : j + 1, :]
        decay = jnp.where(row_id >= col_id, jnp.exp(jnp.minimum(spread, 0.0)), 0.0)
        dmat[j] = decay
        weights = (dot(q2[j], k2[j], NT) * decay).astype(BF16)
        wts[j] = weights
        attended[j] = dot(weights, v2[j], NN)
        growth[j] = jnp.broadcast_to(jnp.exp(col), (TOK, DH))
        qdec_t[j] = (q2[j].astype(F32) * growth[j]).T.astype(BF16)

    for j in range(4):
        gained[j] = gain[mine + j % 2] * og2[j].astype(F32)
    rows_pad[...] = jnp.zeros_like(rows_pad)

    drain_tiles(a_recv.at[2], p_ret)
    for i in range(2):
        chip_state = p_ret[16 * i : 16 * i + 16].reshape(DH, DH)
        states_bf[i] = chip_state.astype(BF16)
        states_bf[2 + i] = (first_decay[i] * chip_state + s_first[i]).astype(BF16)
    for block in range(2):
        square = jnp.zeros((TOK, DH), F32)
        inner = jnp.zeros((TOK, DH), F32)
        for j in (2 * block, 2 * block + 1):
            out = attended[j] + growth[j] * dot(q2[j], states_bf[j], NN)
            attended[j] = out
            square = square + out * out
            inner = inner + gained[j] * out
        sum_send[2 * block : 2 * block + 1, :] = jnp.sum(square.T, axis=0, keepdims=True)
        sum_send[2 * block + 1 : 2 * block + 2, :] = jnp.sum(inner.T, axis=0, keepdims=True)

    place = 2 * y + c
    for dy in Y_STEPS:
        for core in range(2):
            push(sum_send, sum_recv.at[place], 3, 2 * p + core, (y + dy) & (NY - 1))
    push(sum_send, sum_recv.at[place], 3, *partner)
    sum_recv[place] = sum_send[...]
    drain(a_recv.at[3], sum_recv, 2 * NY - 1)
    total = sum_recv[0]
    for i in range(1, 2 * NY):
        total = total + sum_recv[i]
    features = HL * DH * NY
    for block in range(2):
        inv_rms = lax.rsqrt(total[2 * block : 2 * block + 1, :] / features + EPSILON)
        coefficient = total[2 * block + 1 : 2 * block + 2, :] * (inv_rms * inv_rms * inv_rms) / features
        rows_pad[2 * block : 2 * block + 1, :] = inv_rms
        rows_pad[2 * block + 1 : 2 * block + 2, :] = coefficient
    cols_pad[...] = rows_pad[...].T

    for block in range(2):
        inv_wide = jnp.broadcast_to(cols_pad[:, 2 * block : 2 * block + 1], (TOK, DH))
        coef_wide = jnp.broadcast_to(cols_pad[:, 2 * block + 1 : 2 * block + 2], (TOK, DH))
        for j in (2 * block, 2 * block + 1):
            grad = (gained[j] * inv_wide - attended[j] * coef_wide).astype(BF16)
            agrad[j] = grad
            gsum[j] = dot(qdec_t[j], grad, NN)

    for i in range(2):
        u_src[16 * i : 16 * i + 16] = (first_decay[i] * gsum[2 + i] + gsum[i]).reshape(16, 8, DH)
    to_owners(lambda tile: u_src.at[tile], u_all, 4, lambda: u_src[my_tile])

    for j in range(4):
        score = (dot(agrad[j], v2[j], NT) * dmat[j]).astype(BF16)
        qpart[j] = dot(score, k2[j], NN) + growth[j] * dot(agrad[j], states_bf[j], NT)
        kpart[j] = dot(score, q2[j], TN)
        vpart[j] = dot(wts[j], agrad[j], TN)
    swap_parts = [
        swap(3 + n, part.at[pl.ds(theirs, 2)], dst)
        for n, (part, dst) in enumerate(((qpart, qpart_recv), (kpart, kpart_recv), (vpart, vpart_recv)))
    ]
    for i in range(2):
        qg[mine + i] = qpart[mine + i].astype(BF16)

    @pl.when(is_owner)
    def _():
        drain(a_recv.at[4], u_all, CHIPS - 1)

        def body(step, grad):
            chip = CHIPS - 1 - step
            h_src[chip] = grad
            return dec_all[chip] * grad + u_all[chip]

        g_src[...] = lax.fori_loop(0, CHIPS, body, tile_out[...], unroll=4)
        for dz in (6, 5, 7, 4, 8, 3, 9, 2, 10, 1, 11):
            zt = z + dz
            zt = jnp.where(zt >= NZ, zt - NZ, zt)
            push(g_src, g_all.at[c, my_tile], 6, (x * NZ + zt) * 2 + c, y)
        to_chips(lambda chip: push(h_src.at[chip], h_ret.at[my_tile], 5, chip * 2 + c, y))
        h_ret[my_tile] = h_src[p]
        g_all[c, my_tile] = g_src[...]

    for copy in swap_parts:
        copy.wait_recv()
    for i in range(2):
        qg[theirs + i] = qpart_recv[i].astype(BF16)

    drain_tiles(a_recv.at[6], g_all.at[c], OWN_Z)
    line = g_all.at[c, pl.ds(x * OWN_Z, OWN_Z)]
    for dx in X_STEPS[:-1]:
        push(line, line, 6 + dx, (xs[dx] * NZ + z) * 2 + c, y)
    swap_lines = [swap(7, line, line)]

    drain_tiles(a_recv.at[5], h_ret)
    for i in range(2):
        after_second = h_ret[16 * i : 16 * i + 16].reshape(DH, DH)
        after_first = second_decay[i] * after_second + gsum[2 + i]
        h_fwd[i] = jnp.where(first, after_second, after_first)
        grads_bf[mine + i] = jnp.where(first, after_first, after_second).astype(BF16)
    swap_back = swap(6, h_fwd, h_other)

    def finish(h, key_part, value_part):
        kg[h] = (key_part + shrink[h] * dot(v[h], grads_bf[h], NT)).astype(BF16)
        vg[h] = (value_part + shrink[h] * dot(k[h], grads_bf[h], NN)).astype(BF16)

    for i in range(2):
        finish(mine + i, kpart[mine + i], vpart[mine + i])
    swap_back.wait_recv()
    for i in range(2):
        grads_bf[theirs + i] = h_other[i].astype(BF16)
    for i in range(2):
        finish(theirs + i, kpart_recv[i], vpart_recv[i])

    for dx in (1, 3, 2):
        drain(a_recv.at[6 + dx], g_all.at[c], OWN_Z)
        line = g_all.at[c, pl.ds(((x - dx) & (NX - 1)) * OWN_Z, OWN_Z)]
        swap_lines.append(swap(7 + dx, line, line))
    for copy in swap_lines:
        copy.wait_recv()
    sg[...] = g_all[...]

    for copy in (swap_cum, swap_summ, swap_in, *swap_parts, swap_back, *swap_lines):
        copy.wait_send()
    for slot, ref in ((0, dec_all), (1, t_src), (4, u_src)):
        drain_tiles(a_send.at[slot], ref)
    drain(a_send.at[3], sum_recv, 2 * NY - 1)

    @pl.when(is_owner)
    def _():
        for slot in (2, 5):
            drain(a_send.at[slot], p_src, CHIPS - 1)
        drain(a_send.at[6], p_src, NZ - 1)

    for dx in (1, 3, 2):
        drain(a_send.at[6 + dx], p_src, OWN_Z)


def store_kernel(qg, kg, vg, sg, qg_out, kg_out, vg_out, sg_out, sem):
    copies = [pltpu.make_async_copy(sg, sg_out, sem.at[3 * HL])]
    for index, (src, dst) in enumerate(((qg, qg_out), (kg, kg_out), (vg, vg_out))):
        for h in range(HL):
            copies.append(pltpu.make_async_copy(src.at[h], dst.at[:, pl.ds(h * DH, DH)], sem.at[index * HL + h]))
    for copy in copies:
        copy.start()
    for copy in copies:
        copy.wait()


def on_device(query_rows, key_rows, value_rows, log_decay, out_grad, norm_gain, state_in, state_out_grad):
    hbm = pl.BlockSpec(memory_space=pltpu.HBM)
    vmem = pl.BlockSpec(memory_space=pltpu.VMEM)

    def vm(*shape, dtype=F32):
        return pltpu.VMEM(shape, dtype)

    tiles = vm(TILES, 8, DH)
    landing = vm(CHIPS, 8, DH)
    pair = vm(2, DH, DH)
    heads = vm(HL, TOK, DH)
    block_pair = vm(2, TOK, DH)
    heads_bf = vm(HL, TOK, DH, dtype=BF16)
    state = vm(HL, DH, DH)
    state_bf = vm(HL, DH, DH, dtype=BF16)
    dma = pltpu.SemaphoreType.DMA
    rows = jax.ShapeDtypeStruct(query_rows.shape, BF16)
    slab = jax.ShapeDtypeStruct((2, TILES, 8, DH), F32)
    by_head = vm(HL, TOK, DH, dtype=BF16)
    arrays = (
        query_rows, key_rows, value_rows, log_decay, out_grad, norm_gain.reshape(HL, 1, DH),
        state_in.reshape(2 * TILES, 8, DH), state_out_grad.reshape(2 * TILES, 8, DH),
    )
    grads = pl.pallas_call(
        kernel,
        out_shape=(by_head, by_head, by_head, vm(2, TILES, 8, DH)),
        in_specs=[hbm] * 8,
        out_specs=(vmem,) * 4,
        scratch_shapes=[
            heads_bf, heads_bf, heads_bf, heads_bf, vm(HL, 1, DH), vm(HL, TOK), vm(8, DH), vm(8, DH),
            vm(DH, TOK), vm(TOK, DH), vm(8, TOK), vm(DH, TOK), vm(TOK, DH), vm(2, 1, DH), vm(CHIPS, 1, DH),
            vm(4, TOK), vm(2 * NY, 4, TOK), vm(DH, TOK), vm(TOK, DH),
            state, pair, pair, tiles, landing, landing, tiles,
            state, tiles, landing, landing, tiles, pair, pair, vm(8, DH), vm(2, TILES, 8, DH),
            vm(4, 2, TOK, DH), vm(4, 2, TOK, DH), heads_bf, heads_bf, heads_bf, heads_bf,
            state_bf, state_bf, vm(HL, TOK, TOK), vm(HL, TOK, TOK, dtype=BF16), heads, heads, heads, heads, vm(HL, DH, TOK, dtype=BF16), heads_bf,
            heads, heads, heads, block_pair, block_pair, block_pair,
            dma((8,)), dma((11,)), dma((11,)), dma((10,)), dma((10,)),
        ],
        compiler_params=pltpu.CompilerParams(
            collective_id=0, has_side_effects=True, vmem_limit_bytes=32 * 1024 * 1024
        ),
    )(*(pltpu.with_memory_space_constraint(array, pltpu.HBM) for array in arrays))
    qg, kg, vg, sg = pl.pallas_call(
        store_kernel,
        out_shape=(rows, rows, rows, slab),
        in_specs=[vmem] * 4,
        out_specs=(hbm,) * 4,
        scratch_shapes=[dma((3 * HL + 1,))],
        compiler_params=pltpu.CompilerParams(vmem_limit_bytes=4 * 1024 * 1024),
    )(*(pltpu.with_memory_space_constraint(grad, pltpu.VMEM) for grad in grads))
    return qg, kg, vg, sg.reshape(HL, DH, DH)


def solution(mesh):
    wide = P("seq", "head")
    state = P("head", None, None)
    return jax.shard_map(
        on_device,
        mesh=mesh,
        in_specs=(wide, wide, wide, P("head", "seq"), wide, P("head"), state, state),
        out_specs=(wide, wide, wide, state),
        check_vma=False,
    )
```
